128 devices in a mesh: ctx: 64 (over z, x_hi, y, core), head: 2 (over x_lo).
Axes of the slice: x: 4 (x_hi: 2, x_lo: 2; x = x_hi * 2 + x_lo), y: 4, z: 4, core: 2. Of those that a mesh axis runs over, the one named last changes fastest.
Arguments:
- queries: bfloat16 [64, 1024, 2048], P('ctx', None, 'head'), may hold values from -8 to 8
- keys: bfloat16 [64, 1024, 2048], P('ctx', None, 'head'), may hold values from -8 to 8
- values: bfloat16 [64, 1024, 2048], P('ctx', None, 'head'), may hold values from -24 to 24
- w_out: bfloat16 [2048, 4096], P('head'), may hold values from -0.125 to 0.125
Outputs:
- mixed: bfloat16 [64, 1024, 4096], P('ctx', 'head')
The draws below stay inside these ranges and needn't reach their ends.
All inputs are finite; a program needn't handle non-finite values.
Results may differ from the reference program's by a relative error of at most 0.013.
Values may be sent and summed in bfloat16 or wider, within the bound.
No kernel may reach another device: no remote copies, remote signals or barrier semaphores. Data moves between devices by JAX's collectives and lax.ppermute only.
A program may use at most 128 MiB of HBM per device.

```python
import jax
import jax.numpy as jnp
from jax import lax

D = 4096
HD = 128
GROUP = 4
STRIDE = 1024
ROWS = 64
FEAT = 2048
N_HEAD = 2


def draw_queries(key, part):
    shape = (ROWS, STRIDE, FEAT)
    base = jax.random.truncated_normal(jax.random.fold_in(key, 11), -4.0, 4.0, shape, jnp.float32)
    return base.astype(jnp.bfloat16)


def draw_keys(key, part):
    shape = (ROWS, STRIDE, FEAT)
    base = jax.random.truncated_normal(jax.random.fold_in(key, 12), -4.0, 4.0, shape, jnp.float32)
    return base.astype(jnp.bfloat16)


def shard_levels(stream_key, shape, cuts, low, largest):
    level, own = 1.0, jax.random.fold_in(stream_key, 6)
    for dim, blocks in cuts:
        draws = jnp.exp(jax.random.uniform(jax.random.fold_in(own, dim), (blocks,), jnp.float32, low / len(cuts), largest / len(cuts)))
        level = level * jnp.repeat(draws, shape[dim] // blocks).reshape([-1 if axis == dim else 1 for axis in range(len(shape))])
    return level


def noise(stream_key, shape, scale, reach, pieces=(), kind=jnp.bfloat16):
    entries = scale * jax.random.normal(stream_key, shape, jnp.float32)
    if pieces:
        entries = entries * shard_levels(stream_key, shape, pieces, -0.22, 0.18)
    return jnp.clip(entries, -reach, reach).astype(kind)


def setup_inputs(seed: int = 0) -> dict:
    key_of = jax.random.split(jax.random.key(seed), 5)
    queries = draw_queries(jax.random.fold_in(key_of[4], 71), 0)
    keys = draw_keys(jax.random.fold_in(key_of[4], 71), 0)
    values = noise(key_of[2], (ROWS, STRIDE, FEAT), 4.0, 24.0, ((0, 64), (2, 2)))
    w_out = noise(key_of[3], (FEAT, D), FEAT ** -0.5, 0.125, ((0, 2),))
    return {"queries": queries, "keys": keys, "values": values, "w_out": w_out}


masked_score = -1e30


def split_kinds(tensor, parity):
    groups = tensor.shape[2] // (2 * GROUP * HD)
    shaped = tensor.reshape((tensor.shape[0], tensor.shape[1], groups, 2, GROUP, HD))
    return shaped[:, :, :, parity].reshape((tensor.shape[0], tensor.shape[1], groups * GROUP, HD))


def normalized(scores):
    top = jnp.max(scores, axis=-1, keepdims=True)
    expo = jnp.exp(scores - top)
    total = jnp.sum(expo, axis=-1, keepdims=True)
    return (expo / total).astype(jnp.bfloat16)


def reference(queries, keys, values, w_out):
    scale = jnp.float32(1.0 / (HD ** 0.5))
    row_q, row_k, row_v = split_kinds(queries, 0), split_kinds(keys, 0), split_kinds(values, 0)
    col_q, col_k, col_v = split_kinds(queries, 1), split_kinds(keys, 1), split_kinds(values, 1)
    length = STRIDE
    causal_row = lax.broadcasted_iota(jnp.int32, (length, length), 1) <= lax.broadcasted_iota(jnp.int32, (length, length), 0)

    def one_row(triple):
        query_row, key_row, value_row = triple
        scores = jnp.einsum("qhd,khd->hqk", query_row.astype(jnp.float32), key_row.astype(jnp.float32)) * scale
        scores = jnp.where(causal_row, scores, masked_score)
        weights = normalized(scores)
        return jnp.einsum("hqk,khd->qhd", weights.astype(jnp.float32), value_row.astype(jnp.float32)).astype(jnp.bfloat16)

    row_out = lax.map(one_row, (row_q, row_k, row_v))
    causal_col = lax.broadcasted_iota(jnp.int32, (ROWS, ROWS), 1) <= lax.broadcasted_iota(jnp.int32, (ROWS, ROWS), 0)
    scores = jnp.einsum("rchd,schd->chrs", col_q.astype(jnp.float32), col_k.astype(jnp.float32)) * scale
    scores = jnp.where(causal_col, scores, masked_score)
    weights = normalized(scores)
    col_out = jnp.einsum("chrs,schd->rchd", weights.astype(jnp.float32), col_v.astype(jnp.float32)).astype(jnp.bfloat16)
    groups = FEAT // (2 * GROUP * HD)
    joined = jnp.stack([row_out.reshape((ROWS, STRIDE, groups, GROUP, HD)), col_out.reshape((ROWS, STRIDE, groups, GROUP, HD))], axis=3)
    flat = joined.reshape((ROWS * STRIDE, FEAT))
    width = FEAT // N_HEAD
    total = jnp.zeros((ROWS * STRIDE, D), jnp.float32)
    for index in range(N_HEAD):
        term = jnp.dot(flat[:, index * width:(index + 1) * width], w_out[index * width:(index + 1) * width], preferred_element_type=jnp.float32)
        total = total + lax.optimization_barrier(term.astype(jnp.bfloat16)).astype(jnp.float32)
    return total.astype(jnp.bfloat16).reshape((ROWS, STRIDE, D))
```

```python
import functools
import itertools
import math

import jax
import jax.numpy as jnp
from jax import lax
from jax.experimental import pallas as pl
from jax.experimental.pallas import tpu as pltpu
from jax.sharding import PartitionSpec as P

HD = 128
GROUP = 4
LOCAL = GROUP * HD
LENGTH = 1024
ROWS = 64
HALF = LENGTH // 2
WIDTH = 4096
BLOCK = 256
SCALE = math.log2(math.e) / math.sqrt(HD)
MASKED = -1e30
VMEM = 60 << 20

GATHER_GROUPS = [
    [z * 16 + x_hi * 8 + rest for z, rest in itertools.product(range(4), range(8))]
    for x_hi in range(2)
]
GATHER_SIZE = 32


def softmax_rows(scores):
    top = jnp.max(scores, axis=-1, keepdims=True)
    expo = jnp.exp2((scores - top) * SCALE)
    total = jnp.sum(expo, axis=-1, keepdims=True)
    return expo.astype(jnp.bfloat16), total


def dot_nt(a, b):
    return lax.dot_general(a, b, (((1,), (1,)), ((), ())), preferred_element_type=jnp.float32)


def dot_nn(a, b):
    return jnp.dot(a, b, preferred_element_type=jnp.float32)


def row_kernel(q_ref, k_ref, v_ref, own_ref, other_ref):
    me = lax.axis_index("head")
    lower = lax.broadcasted_iota(jnp.int32, (BLOCK, BLOCK), 1) <= lax.broadcasted_iota(
        jnp.int32, (BLOCK, BLOCK), 0
    )
    per_half = HALF // BLOCK
    for i in range(LENGTH // BLOCK):
        q = q_ref[0, i * BLOCK : (i + 1) * BLOCK, :]
        end = (i + 1) * BLOCK
        diag = jnp.where(lower, dot_nt(q, k_ref[0, i * BLOCK : end, :]), MASKED)
        if i:
            scores = jnp.concatenate([dot_nt(q, k_ref[0, : i * BLOCK, :]), diag], axis=1)
        else:
            scores = diag
        probs, total = softmax_rows(scores)
        out = (dot_nn(probs, v_ref[0, :end, :]) / total).astype(jnp.bfloat16)
        at = pl.ds((i % per_half) * BLOCK, BLOCK)

        @pl.when(me == i // per_half)
        def _():
            own_ref[at, :] = out

        @pl.when(me != i // per_half)
        def _():
            other_ref[at, :] = out


def row_attention(queries, keys, values):
    spec = pl.BlockSpec((1, LENGTH, HD), lambda h: (0, 0, h))
    out_spec = pl.BlockSpec((HALF, HD), lambda h: (0, h))
    shape = jax.ShapeDtypeStruct((HALF, LOCAL), jnp.bfloat16)
    return pl.pallas_call(
        row_kernel,
        grid=(GROUP,),
        in_specs=[spec] * 3,
        out_specs=[out_spec] * 2,
        out_shape=[shape, shape],
        compiler_params=pltpu.CompilerParams(vmem_limit_bytes=VMEM),
        cost_estimate=pl.CostEstimate(
            flops=4 * GROUP * LENGTH * LENGTH * HD,
            transcendentals=GROUP * LENGTH * LENGTH,
            bytes_accessed=4 * 2 * LENGTH * LOCAL,
        ),
        name="row_attention",
    )(queries, keys, values)


COLS = 16
SUB = 16
TOKENS = SUB * COLS


def column_kernel(x_ref, o_ref):
    to = lax.broadcasted_iota(jnp.int32, (TOKENS, TOKENS), 0)
    of = lax.broadcasted_iota(jnp.int32, (TOKENS, TOKENS), 1)
    swap = ((to % SUB) * COLS + to // SUB == of).astype(jnp.bfloat16)
    back = ((to % COLS) * SUB + to // COLS == of).astype(jnp.bfloat16)
    blocks = ROWS // SUB
    regrouped = []
    for b in range(blocks):
        x = x_ref[b * SUB : (b + 1) * SUB]
        parts = [x[:, t * COLS : (t + 1) * COLS, :].reshape(TOKENS, HD) for t in range(3)]
        regrouped.append(dot_nn(swap, jnp.concatenate(parts, axis=1)).astype(jnp.bfloat16))
    span = TOKENS // blocks
    row_of = (to // span) * SUB + to % SUB
    row_at = (of // span) * SUB + of % SUB
    allowed = ((to // SUB) % (span // SUB) == (of // SUB) % (span // SUB)) & (row_at <= row_of)
    outs = []
    for g in range(TOKENS // span):
        mine = jnp.concatenate([y[g * span : (g + 1) * span] for y in regrouped], axis=0)
        q, k, v = (mine[:, t * HD : (t + 1) * HD] for t in range(3))
        probs, total = softmax_rows(jnp.where(allowed, dot_nt(q, k), MASKED))
        outs.append((dot_nn(probs, v) / total).astype(jnp.bfloat16))
    for b in range(blocks):
        y = jnp.concatenate([o[b * span : (b + 1) * span] for o in outs], axis=0)
        z = dot_nn(back, y).astype(jnp.bfloat16)
        o_ref[b * SUB : (b + 1) * SUB] = z.reshape(SUB, COLS, HD)


def column_attention(x):
    return pl.pallas_call(
        column_kernel,
        grid=(GROUP,),
        in_specs=[pl.BlockSpec((ROWS, 3 * COLS, HD), lambda h: (0, 0, h))],
        out_specs=pl.BlockSpec((ROWS, COLS, HD), lambda h: (0, 0, h)),
        out_shape=jax.ShapeDtypeStruct((ROWS, COLS, LOCAL), jnp.bfloat16),
        compiler_params=pltpu.CompilerParams(vmem_limit_bytes=VMEM),
        cost_estimate=pl.CostEstimate(
            flops=4 * GROUP * ROWS * COLS * TOKENS * HD,
            transcendentals=GROUP * ROWS * COLS * TOKENS,
            bytes_accessed=4 * 2 * ROWS * COLS * LOCAL,
        ),
        name="column_attention",
    )(x)


TILE = 512


def row_project_kernel(a_ref, b_ref, w_ref, u_ref, o_ref):
    o_ref[...] = dot_nn(a_ref[...], w_ref[...]) + dot_nn(b_ref[...], u_ref[...])


def row_project(own, other, w_own, w_other):
    whole = pl.BlockSpec((HALF, LOCAL), lambda n: (0, 0))
    w_spec = pl.BlockSpec((LOCAL, TILE), lambda n: (0, n))
    return pl.pallas_call(
        row_project_kernel,
        grid=(WIDTH // TILE,),
        in_specs=[whole, whole, w_spec, w_spec],
        out_specs=pl.BlockSpec((HALF, TILE), lambda n: (0, n)),
        out_shape=jax.ShapeDtypeStruct((HALF, WIDTH), jnp.float32),
        compiler_params=pltpu.CompilerParams(vmem_limit_bytes=VMEM),
        cost_estimate=pl.CostEstimate(
            flops=4 * HALF * LOCAL * WIDTH, transcendentals=0, bytes_accessed=16 << 20
        ),
        name="row_project",
    )(own, other, w_own, w_other)


def column_project_kernel(acc_ref, a_ref, w_ref, u_ref, o_ref):
    me = lax.axis_index("head")
    own = a_ref[:, me].reshape(HALF, LOCAL)
    other = a_ref[:, 1 - me].reshape(HALF, LOCAL)
    total = acc_ref[...] + dot_nn(own, w_ref[...]) + dot_nn(other, u_ref[...])
    o_ref[0] = total.astype(jnp.bfloat16)


def column_project(acc, attended, w_own, w_other):
    w_spec = pl.BlockSpec((LOCAL, TILE), lambda n: (1, n))
    return pl.pallas_call(
        column_project_kernel,
        grid=(WIDTH // TILE,),
        in_specs=[
            pl.BlockSpec((HALF, TILE), lambda n: (0, n)),
            pl.BlockSpec((ROWS, 2, 8, LOCAL), lambda n: (0, 0, 0, 0)),
            w_spec,
            w_spec,
        ],
        out_specs=pl.BlockSpec((1, HALF, TILE), lambda n: (0, 0, n)),
        out_shape=jax.ShapeDtypeStruct((1, HALF, WIDTH), jnp.bfloat16),
        compiler_params=pltpu.CompilerParams(vmem_limit_bytes=VMEM),
        cost_estimate=pl.CostEstimate(
            flops=4 * HALF * LOCAL * WIDTH, transcendentals=0, bytes_accessed=20 << 20
        ),
        name="column_project",
    )(acc, attended, w_own, w_other)


SWAP = [(0, 1), (1, 0)]


def other_weights(w_out):
    ctx = lax.axis_index("ctx")
    place = (ctx // 16) * 8 + ctx % 8
    rows = w_out.shape[0] // GATHER_SIZE
    piece = lax.dynamic_slice_in_dim(w_out, place * rows, rows, 0)
    piece = lax.ppermute(piece, "head", SWAP)
    return lax.all_gather(piece, "ctx", axis=0, tiled=True, axis_index_groups=GATHER_GROUPS)


def packed(tensor):
    x = tensor[0, :, LOCAL:].reshape(2, ROWS, 8, LOCAL)
    return jnp.swapaxes(x, 0, 1).reshape(ROWS, COLS, LOCAL)


def on_device(queries, keys, values, w_out):
    sent = jnp.concatenate([packed(queries), packed(keys), packed(values)], axis=1)
    arrived = lax.all_to_all(sent, "ctx", split_axis=0, concat_axis=0, tiled=True)
    w_other = other_weights(w_out)
    row_own, row_away = row_attention(queries, keys, values)
    arrived, row_own, row_away = lax.optimization_barrier((arrived, row_own, row_away))
    row_other = lax.ppermute(row_away, "head", SWAP)
    acc = row_project(row_own, row_other, w_out, w_other)
    col = column_attention(arrived).reshape(2 * ROWS, 8, LOCAL)
    col = lax.all_to_all(col, ("ctx", "head"), split_axis=0, concat_axis=0, tiled=True)
    return column_project(acc, col.reshape(ROWS, 2, 8, LOCAL), w_out, w_other)


def solution(mesh):
    return jax.shard_map(
        on_device,
        mesh=mesh,
        in_specs=(
            P("ctx", None, "head"),
            P("ctx", None, "head"),
            P("ctx", None, "head"),
            P("head", None),
        ),
        out_specs=P("ctx", "head", None),
        check_vma=False,
    )
```

```python
import itertools
import math

import jax
import jax.numpy as jnp
from jax import lax
from jax.experimental import pallas as pl
from jax.experimental.pallas import tpu as pltpu
from jax.sharding import PartitionSpec as P

HD = 128
GROUP = 4
LOCAL = GROUP * HD
LENGTH = 1024
ROWS = 64
HALF = LENGTH // 2
WIDTH = 4096
BLOCK = 256
SCALE = math.log2(math.e) / math.sqrt(HD)
MASKED = -1e30
SMALL_VMEM = 16 << 20
COST = pl.CostEstimate(flops=1 << 20, transcendentals=0, bytes_accessed=1 << 10)
LONG = pl.CostEstimate(flops=1 << 38, transcendentals=0, bytes_accessed=1 << 20)

PLACES = list(itertools.product(range(4), range(4), range(4), range(2)))
HALF_WIDTH = WIDTH // 2
PIECE = LENGTH // 4


def index_of(x, y, z, core):
    return (((z % 4) * 2 + (x % 4) // 2) * 4 + y % 4) * 4 + core * 2 + x % 2


def pair(at, core):
    return at + 1 if at % 2 == core else at - 1


def moves(step):
    return [(index_of(*place), index_of(*step(*place))) for place in PLACES]


ALONG_X = moves(lambda x, y, z, core: (x + 1 - 2 * core, y, z, core))
ALONG_Y = moves(lambda x, y, z, core: (x, pair(y, core), z, core))
ALONG_Z = moves(lambda x, y, z, core: (x, y, pair(z, core), core))
ALONG_N = moves(lambda x, y, z, core: (x - 1 + 2 * (x % 2), y, z, core))
TO_CORE = moves(lambda x, y, z, core: (x, y, z, 1 - core))
TO_HEAD = moves(lambda x, y, z, core: (x + 1 - 2 * (x % 2), y, z, core))


def position():
    ctx = lax.axis_index("ctx")
    return ctx & 1, (ctx >> 1) & 1, (ctx >> 4) & 1


def permute(x, pairs):
    return lax.ppermute(x, ("ctx", "head"), pairs)


def in_hbm(x):
    return pltpu.with_memory_space_constraint(x, pltpu.HBM)


def softmax_rows(scores):
    top = jnp.max(scores, axis=-1, keepdims=True)
    expo = jnp.exp2((scores - top) * SCALE)
    total = jnp.sum(expo, axis=-1, keepdims=True)
    return expo.astype(jnp.bfloat16), total


def dot_nt(a, b):
    return lax.dot_general(a, b, (((1,), (1,)), ((), ())), preferred_element_type=jnp.float32)


def dot_nn(a, b):
    return jnp.dot(a, b, preferred_element_type=jnp.float32)


def row_kernel(q_ref, k_ref, v_ref, own_ref, other_ref):
    me = lax.axis_index("head")
    lower = lax.broadcasted_iota(jnp.int32, (BLOCK, BLOCK), 1) <= lax.broadcasted_iota(
        jnp.int32, (BLOCK, BLOCK), 0
    )
    per_half = HALF // BLOCK
    other_ref[HALF:] = jnp.zeros((HALF, HD), jnp.bfloat16)
    for i in range(LENGTH // BLOCK):
        q = q_ref[0, i * BLOCK : (i + 1) * BLOCK, :]
        end = (i + 1) * BLOCK
        diag = jnp.where(lower, dot_nt(q, k_ref[0, i * BLOCK : end, :]), MASKED)
        if i:
            scores = jnp.concatenate([dot_nt(q, k_ref[0, : i * BLOCK, :]), diag], axis=1)
        else:
            scores = diag
        probs, total = softmax_rows(scores)
        out = (dot_nn(probs, v_ref[0, :end, :]) / total).astype(jnp.bfloat16)
        at = pl.ds((i % per_half) * BLOCK, BLOCK)

        @pl.when(me == i // per_half)
        def _():
            own_ref[at, :] = out

        @pl.when(me != i // per_half)
        def _():
            other_ref[at, :] = out


def row_attention(queries, keys, values):
    spec = pl.BlockSpec((1, LENGTH, HD), lambda h: (0, 0, h))
    return pl.pallas_call(
        row_kernel,
        grid=(GROUP,),
        in_specs=[spec] * 3,
        out_specs=[
            pl.BlockSpec((HALF, HD), lambda h: (0, h)),
            pl.BlockSpec((2 * HALF, HD), lambda h: (0, h)),
        ],
        out_shape=[
            pltpu.HBM((HALF, LOCAL), jnp.bfloat16),
            pltpu.HBM((2 * HALF, LOCAL), jnp.bfloat16),
        ],
        compiler_params=pltpu.CompilerParams(vmem_limit_bytes=SMALL_VMEM),
        cost_estimate=LONG,
        name="row_attention",
    )(in_hbm(queries), in_hbm(keys), in_hbm(values))


COLS = 16
SUB = 16
TOKENS = SUB * COLS


def column_kernel(x_ref, o_ref):
    to = lax.broadcasted_iota(jnp.int32, (TOKENS, TOKENS), 0)
    of = lax.broadcasted_iota(jnp.int32, (TOKENS, TOKENS), 1)
    swap = ((to % SUB) * COLS + to // SUB == of).astype(jnp.bfloat16)
    back = ((to % COLS) * SUB + to // COLS == of).astype(jnp.bfloat16)
    blocks = ROWS // SUB
    regrouped = []
    for b in range(blocks):
        x = x_ref[b * SUB : (b + 1) * SUB]
        parts = [x[:, t * COLS : (t + 1) * COLS, :].reshape(TOKENS, HD) for t in range(3)]
        regrouped.append(dot_nn(swap, jnp.concatenate(parts, axis=1)).astype(jnp.bfloat16))
    span = TOKENS // blocks
    row_of = (to // span) * SUB + to % SUB
    row_at = (of // span) * SUB + of % SUB
    allowed = ((to // SUB) % (span // SUB) == (of // SUB) % (span // SUB)) & (row_at <= row_of)
    outs = []
    for g in range(TOKENS // span):
        mine = jnp.concatenate([y[g * span : (g + 1) * span] for y in regrouped], axis=0)
        q, k, v = (mine[:, t * HD : (t + 1) * HD] for t in range(3))
        probs, total = softmax_rows(jnp.where(allowed, dot_nt(q, k), MASKED))
        outs.append((dot_nn(probs, v) / total).astype(jnp.bfloat16))
    for b in range(blocks):
        y = jnp.concatenate([o[b * span : (b + 1) * span] for o in outs], axis=0)
        z = dot_nn(back, y).astype(jnp.bfloat16)
        o_ref[b * SUB : (b + 1) * SUB] = z.reshape(SUB, COLS, HD)


def column_attention(x):
    return pl.pallas_call(
        column_kernel,
        grid=(GROUP,),
        in_specs=[pl.BlockSpec((ROWS, 3 * COLS, HD), lambda h: (0, 0, h))],
        out_specs=pl.BlockSpec((ROWS, COLS, HD), lambda h: (0, 0, h)),
        out_shape=pltpu.HBM((ROWS, COLS, LOCAL), jnp.bfloat16),
        compiler_params=pltpu.CompilerParams(vmem_limit_bytes=SMALL_VMEM),
        cost_estimate=COST,
        name="column_attention",
    )(x)


TILE = 512
TILES = WIDTH // TILE


def tile_of(n, core):
    return lax.rem(n + core * (TILES // 2), TILES)


def join_kernel(s_ref, row_own, row_other, x_ref, a_ref):
    mine, me = 2 * s_ref[1] + s_ref[2], s_ref[3]
    a_ref[:, :LOCAL] = row_own[...]
    a_ref[:, LOCAL : 2 * LOCAL] = x_ref[:, me].reshape(HALF, LOCAL)
    other = x_ref[:, 1 - me].reshape(HALF, LOCAL)
    quarters = [row_other[:, :PIECE], row_other[:, PIECE:], other[:, :PIECE], other[:, PIECE:]]
    for i in range(4):
        picked = quarters[0]
        for q in range(1, 4):
            picked = jnp.where(lax.bitwise_xor(mine, i) == q, quarters[q], picked)
        a_ref[:, 2 * LOCAL + i * PIECE : 2 * LOCAL + (i + 1) * PIECE] = picked


def join(place, row_own, row_other, attended):
    return pl.pallas_call(
        join_kernel,
        grid=(1,),
        in_specs=[
            pl.BlockSpec(memory_space=pltpu.SMEM),
            pl.BlockSpec((HALF, LOCAL), lambda n: (0, 0)),
            pl.BlockSpec((HALF, LOCAL), lambda n: (0, 0)),
            pl.BlockSpec((ROWS, 2, 8, LOCAL), lambda n: (0, 0, 0, 0)),
        ],
        out_shape=jax.ShapeDtypeStruct((HALF, 4 * LOCAL), jnp.bfloat16),
        compiler_params=pltpu.CompilerParams(vmem_limit_bytes=SMALL_VMEM),
        cost_estimate=LONG,
        name="join",
    )(place, in_hbm(row_own), row_other, attended)


def project_kernel(s_ref, a_ref, w_ref, *refs):
    near, far, o_ref = refs[:4], refs[4:8], refs[8]
    n = pl.program_id(0)

    def product(pieces):
        weights = jnp.concatenate([w_ref[...], *[p[...] for p in pieces]], axis=0)
        o_ref[0] = dot_nn(a_ref[...], weights).astype(jnp.bfloat16)

    @pl.when(n < TILES // 2)
    def _():
        product(near)

    @pl.when(n >= TILES // 2)
    def _():
        product(far)


def project(place, joined, w_own, pieces):
    half = TILES // 2
    near = pl.BlockSpec((PIECE, TILE), lambda n, s: (0, jnp.minimum(n, half - 1)))
    far = pl.BlockSpec((PIECE, TILE), lambda n, s: (0, jnp.maximum(n - half, 0)))
    return pl.pallas_call(
        project_kernel,
        grid_spec=pltpu.PrefetchScalarGridSpec(
            num_scalar_prefetch=1,
            grid=(TILES,),
            in_specs=[
                pl.BlockSpec((HALF, 4 * LOCAL), lambda n, s: (0, 0)),
                pl.BlockSpec((2 * LOCAL, TILE), lambda n, s: (0, tile_of(n, s[0]))),
                *[near] * 4,
                *[far] * 4,
            ],
            out_specs=pl.BlockSpec((1, HALF, TILE), lambda n, s: (0, 0, tile_of(n, s[0]))),
        ),
        out_shape=jax.ShapeDtypeStruct((1, HALF, WIDTH), jnp.bfloat16),
        compiler_params=pltpu.CompilerParams(vmem_limit_bytes=24 << 20),
        cost_estimate=COST,
        name="project",
    )(place, joined, in_hbm(w_own), *map(in_hbm, pieces))


def slice_kernel(s_ref, w_ref, x_ref, y_ref, buf, in_sems, out_sems):
    columns = pl.ds(pl.multiple_of(s_ref[0] * HALF_WIDTH, HALF_WIDTH), HALF_WIDTH)
    outs = (x_ref, y_ref)
    mine = 2 * s_ref[1] + s_ref[2]
    loads, stores = [], []
    for i, quarter in enumerate((mine, 3 - mine)):
        start = pl.multiple_of(quarter * PIECE, PIECE)
        loads.append(
            pltpu.make_async_copy(w_ref.at[pl.ds(start, PIECE), columns], buf.at[i], in_sems.at[i])
        )
        stores.append(pltpu.make_async_copy(buf.at[i], outs[i], out_sems.at[i]))
    for load in loads:
        load.start()
    for load, store in zip(loads, stores):
        load.wait()
        store.start()
    for store in stores:
        store.wait()


def slices(place, w_out):
    shape = pltpu.HBM((PIECE, HALF_WIDTH), jnp.bfloat16)
    return pl.pallas_call(
        slice_kernel,
        in_specs=[pl.BlockSpec(memory_space=pltpu.SMEM), pl.BlockSpec(memory_space=pl.ANY)],
        out_specs=[pl.BlockSpec(memory_space=pl.ANY)] * 2,
        out_shape=[shape, shape],
        scratch_shapes=[
            pltpu.VMEM((2, PIECE, HALF_WIDTH), jnp.bfloat16),
            pltpu.SemaphoreType.DMA((2,)),
            pltpu.SemaphoreType.DMA((2,)),
        ],
        compiler_params=pltpu.CompilerParams(vmem_limit_bytes=SMALL_VMEM),
        cost_estimate=COST,
        name="slices",
    )(place, in_hbm(w_out))


PACK_STEPS = 4


def pack_kernel(q_ref, k_ref, v_ref, o_ref, buf, in_sems, out_sems):
    step = ROWS // PACK_STEPS
    loads, stores = [], []
    for n in range(PACK_STEPS):
        at = pl.ds(n * step, step)
        loads.append(
            [
                pltpu.make_async_copy(
                    ref.at[0, half, at, :, pl.ds(LOCAL, LOCAL)],
                    buf.at[at, 2 * t + half],
                    in_sems.at[n, 2 * t + half],
                )
                for t, ref in enumerate((q_ref, k_ref, v_ref))
                for half in range(2)
            ]
        )
        stores.append(pltpu.make_async_copy(buf.at[at], o_ref.at[at], out_sems.at[n]))
    for group in loads:
        for load in group:
            load.start()
    for group, store in zip(loads, stores):
        for load in group:
            load.wait()
        store.start()
    for store in stores:
        store.wait()


def packed(*tensors):
    return pl.pallas_call(
        pack_kernel,
        in_specs=[pl.BlockSpec(memory_space=pl.ANY)] * 3,
        out_specs=pl.BlockSpec(memory_space=pl.ANY),
        out_shape=pltpu.HBM((ROWS, 6, 8, LOCAL), jnp.bfloat16),
        scratch_shapes=[
            pltpu.VMEM((ROWS, 6, 8, LOCAL), jnp.bfloat16),
            pltpu.SemaphoreType.DMA((PACK_STEPS, 6)),
            pltpu.SemaphoreType.DMA((PACK_STEPS,)),
        ],
        compiler_params=pltpu.CompilerParams(vmem_limit_bytes=SMALL_VMEM),
        cost_estimate=COST,
        name="pack",
    )(*[in_hbm(t.reshape(1, 2, ROWS, 8, 2 * LOCAL)) for t in tensors]).reshape(ROWS, 3 * COLS, LOCAL)


def on_device(queries, keys, values, w_out):
    place = jnp.stack([*position(), lax.axis_index("head")])
    pieces, *col_qkv = lax.optimization_barrier((slices(place, w_out), queries, keys, values))
    mine = permute(pieces[0], ALONG_X)
    sent = packed(*col_qkv)
    arrived = lax.all_to_all(sent, "ctx", split_axis=0, concat_axis=0, tiled=True)
    mine, away, *row_qkv = lax.optimization_barrier((mine, pieces[1], queries, keys, values))
    row_own, row_away = row_attention(*row_qkv)
    mine, away, row_own, row_away = lax.optimization_barrier((mine, away, row_own, row_away))
    quarters = [mine, permute(mine, ALONG_Z), permute(mine, ALONG_Y), permute(away, ALONG_N)]
    row_other = permute(row_away, TO_HEAD)
    col = column_attention(arrived)
    *quarters, row_other, _ = lax.optimization_barrier((*quarters, row_other, col))
    quarters += [permute(quarter, TO_CORE) for quarter in quarters]
    col = col.reshape(2 * ROWS, 8, LOCAL)
    col = lax.all_to_all(col, ("ctx", "head"), split_axis=0, concat_axis=0, tiled=True)
    joined = join(place, row_own, row_other, col.reshape(ROWS, 2, 8, LOCAL))
    return project(place, joined, w_out, quarters)


def solution(mesh):
    return jax.shard_map(
        on_device,
        mesh=mesh,
        in_specs=(
            P("ctx", None, "head"),
            P("ctx", None, "head"),
            P("ctx", None, "head"),
            P("head", None),
        ),
        out_specs=P("ctx", "head", None),
        check_vma=False,
    )
```

```python
import functools
import itertools
import math

import jax
import jax.numpy as jnp
from jax import lax
from jax.experimental import pallas as pl
from jax.experimental.pallas import tpu as pltpu
from jax.sharding import PartitionSpec as P

HD = 128
GROUP = 4
LOCAL = GROUP * HD
LENGTH = 1024
ROWS = 64
HALF = LENGTH // 2
WIDTH = 4096
BLOCK = 256
SCALE = math.log2(math.e) / math.sqrt(HD)
MASKED = -1e30
SMALL_VMEM = 16 << 20
COST = pl.CostEstimate(flops=1 << 20, transcendentals=0, bytes_accessed=1 << 10)
LONG = pl.CostEstimate(flops=1 << 38, transcendentals=0, bytes_accessed=1 << 20)

PLACES = list(itertools.product(range(4), range(4), range(4), range(2)))
HALF_WIDTH = WIDTH // 2
PIECE = LENGTH // 4


def index_of(x, y, z, core):
    return (((z % 4) * 2 + (x % 4) // 2) * 4 + y % 4) * 4 + core * 2 + x % 2


def pair(at, core):
    return at + 1 if at % 2 == core else at - 1


def moves(step):
    return [(index_of(*place), index_of(*step(*place))) for place in PLACES]


ALONG_X = moves(lambda x, y, z, core: (x + 1 - 2 * core, y, z, core))
ALONG_Y = moves(lambda x, y, z, core: (x, pair(y, core), z, core))
ALONG_Z = moves(lambda x, y, z, core: (x, y, pair(z, core), core))
ALONG_N = moves(lambda x, y, z, core: (x - 1 + 2 * (x % 2), y, z, core))
TO_CORE = moves(lambda x, y, z, core: (x, y, z, 1 - core))
TO_HEAD = moves(lambda x, y, z, core: (x + 1 - 2 * (x % 2), y, z, core))


def position():
    ctx = lax.axis_index("ctx")
    return ctx & 1, (ctx >> 1) & 1, (ctx >> 4) & 1


def permute(x, pairs):
    return lax.ppermute(x, ("ctx", "head"), pairs)


def in_hbm(x):
    return pltpu.with_memory_space_constraint(x, pltpu.HBM)


def softmax_rows(scores):
    top = jnp.max(scores, axis=-1, keepdims=True)
    expo = jnp.exp2((scores - top) * SCALE)
    total = jnp.sum(expo, axis=-1, keepdims=True)
    return expo.astype(jnp.bfloat16), total


def dot_nt(a, b):
    return lax.dot_general(a, b, (((1,), (1,)), ((), ())), preferred_element_type=jnp.float32)


def dot_nn(a, b):
    return jnp.dot(a, b, preferred_element_type=jnp.float32)


def row_kernel(q_ref, k_ref, v_ref, own_ref, other_ref):
    me = lax.axis_index("head")
    lower = lax.broadcasted_iota(jnp.int32, (BLOCK, BLOCK), 1) <= lax.broadcasted_iota(
        jnp.int32, (BLOCK, BLOCK), 0
    )
    per_half = HALF // BLOCK
    other_ref[HALF:] = jnp.zeros((HALF, HD), jnp.bfloat16)
    for i in range(LENGTH // BLOCK):
        q = q_ref[0, i * BLOCK : (i + 1) * BLOCK, :]
        end = (i + 1) * BLOCK
        diag = jnp.where(lower, dot_nt(q, k_ref[0, i * BLOCK : end, :]), MASKED)
        if i:
            scores = jnp.concatenate([dot_nt(q, k_ref[0, : i * BLOCK, :]), diag], axis=1)
        else:
            scores = diag
        probs, total = softmax_rows(scores)
        out = (dot_nn(probs, v_ref[0, :end, :]) / total).astype(jnp.bfloat16)
        at = pl.ds((i % per_half) * BLOCK, BLOCK)

        @pl.when(me == i // per_half)
        def _():
            own_ref[at, :] = out

        @pl.when(me != i // per_half)
        def _():
            other_ref[at, :] = out


def row_attention(queries, keys, values):
    spec = pl.BlockSpec((1, LENGTH, HD), lambda h: (0, 0, h))
    return pl.pallas_call(
        row_kernel,
        grid=(GROUP,),
        in_specs=[spec] * 3,
        out_specs=[
            pl.BlockSpec((HALF, HD), lambda h: (0, h)),
            pl.BlockSpec((2 * HALF, HD), lambda h: (0, h)),
        ],
        out_shape=[
            pltpu.HBM((HALF, LOCAL), jnp.bfloat16),
            pltpu.HBM((2 * HALF, LOCAL), jnp.bfloat16),
        ],
        compiler_params=pltpu.CompilerParams(vmem_limit_bytes=SMALL_VMEM),
        cost_estimate=LONG,
        name="row_attention",
    )(in_hbm(queries), in_hbm(keys), in_hbm(values))


COLS = 16
SUB = 16
TOKENS = SUB * COLS
AT_ONCE = 2


def column_kernel(x_ref, o_ref):
    to = lax.broadcasted_iota(jnp.int32, (TOKENS, TOKENS), 0)
    of = lax.broadcasted_iota(jnp.int32, (TOKENS, TOKENS), 1)
    swap = ((to % SUB) * COLS + to // SUB == of).astype(jnp.bfloat16)
    back = ((to % COLS) * SUB + to // COLS == of).astype(jnp.bfloat16)
    blocks = ROWS // SUB
    heads = o_ref.shape[2] // HD
    width = heads * HD
    regrouped = []
    for b in range(blocks):
        x = x_ref[b * SUB : (b + 1) * SUB]
        parts = [x[:, t * COLS : (t + 1) * COLS, :].reshape(TOKENS, width) for t in range(3)]
        regrouped.append(dot_nn(swap, jnp.concatenate(parts, axis=1)).astype(jnp.bfloat16))
    span = TOKENS // blocks
    row_of = (to // span) * SUB + to % SUB
    row_at = (of // span) * SUB + of % SUB
    allowed = ((to // SUB) % (span // SUB) == (of // SUB) % (span // SUB)) & (row_at <= row_of)
    outs = []
    for g in range(TOKENS // span):
        mine = jnp.concatenate([y[g * span : (g + 1) * span] for y in regrouped], axis=0)
        across = []
        for h in range(heads):
            q, k, v = (mine[:, t * width + h * HD : t * width + (h + 1) * HD] for t in range(3))
            probs, total = softmax_rows(jnp.where(allowed, dot_nt(q, k), MASKED))
            across.append((dot_nn(probs, v) / total).astype(jnp.bfloat16))
        outs.append(jnp.concatenate(across, axis=1))
    for b in range(blocks):
        y = jnp.concatenate([o[b * span : (b + 1) * span] for o in outs], axis=0)
        z = dot_nn(back, y).astype(jnp.bfloat16)
        o_ref[b * SUB : (b + 1) * SUB] = z.reshape(SUB, COLS, width)


def column_attention(x):
    return pl.pallas_call(
        column_kernel,
        grid=(GROUP // AT_ONCE,),
        in_specs=[pl.BlockSpec((ROWS, 3 * COLS, AT_ONCE * HD), lambda h: (0, 0, h))],
        out_specs=pl.BlockSpec((ROWS, COLS, AT_ONCE * HD), lambda h: (0, 0, h)),
        out_shape=pltpu.HBM((ROWS, COLS, LOCAL), jnp.bfloat16),
        compiler_params=pltpu.CompilerParams(vmem_limit_bytes=SMALL_VMEM),
        cost_estimate=COST,
        name="column_attention",
    )(x)


TILE = 1024
TILES = WIDTH // TILE
CHUNK = 512
CHUNKS = WIDTH // CHUNK
WHOLE = pl.BlockSpec(memory_space=pltpu.VMEM)
ANYWHERE = pl.BlockSpec(memory_space=pl.ANY)


def own_rows_kernel(a_ref, w_ref, o_ref):
    o_ref[...] = dot_nn(a_ref[...], w_ref[...]).astype(jnp.bfloat16)


def project_own_rows(own, w_own):
    return pl.pallas_call(
        own_rows_kernel,
        grid=(TILES,),
        in_specs=[
            pl.BlockSpec((HALF, LOCAL), lambda n: (0, 0)),
            pl.BlockSpec((LOCAL, TILE), lambda n: (0, n)),
        ],
        out_specs=pl.BlockSpec((HALF, TILE), lambda n: (0, n)),
        out_shape=pltpu.HBM((HALF, WIDTH), jnp.bfloat16),
        compiler_params=pltpu.CompilerParams(vmem_limit_bytes=SMALL_VMEM),
        cost_estimate=COST,
        name="own_rows",
    )(in_hbm(own), in_hbm(w_own))


def join_kernel(s_ref, x_ref, a_ref):
    me = s_ref[3]
    a_ref[:, :LOCAL] = x_ref[:, me].reshape(HALF, LOCAL)
    a_ref[:, LOCAL:] = x_ref[:, 1 - me].reshape(HALF, LOCAL)


def join(place, attended):
    return pl.pallas_call(
        join_kernel,
        in_specs=[pl.BlockSpec(memory_space=pltpu.SMEM), WHOLE],
        out_specs=WHOLE,
        out_shape=jax.ShapeDtypeStruct((HALF, 2 * LOCAL), jnp.bfloat16),
        compiler_params=pltpu.CompilerParams(vmem_limit_bytes=SMALL_VMEM),
        cost_estimate=LONG,
        name="join",
    )(place, attended)


def project_kernel(s_ref, x_ref, y_ref, acc_ref, w_ref, *refs):
    pieces, o_ref = refs[:8], refs[8]
    a_buf, w_buf, acc_buf, o_buf, load_sems, store_sems = refs[9:]
    core, mine = s_ref[0], 2 * s_ref[1] + s_ref[2]
    half = CHUNKS // 2

    def columns_of(n):
        at = lax.rem(n + core * half, CHUNKS)
        return pl.ds(pl.multiple_of(at * CHUNK, CHUNK), CHUNK)

    def loads_of(n):
        columns = columns_of(n)
        there = pl.ds(n % half * CHUNK, CHUNK)
        rows = pl.ds(LOCAL, LOCAL)
        loads = [
            pltpu.make_async_copy(acc_ref.at[:, columns], acc_buf.at[n], load_sems.at[n, 0]),
            pltpu.make_async_copy(
                w_ref.at[rows, columns], w_buf.at[n, pl.ds(0, LOCAL)], load_sems.at[n, 1]
            ),
        ]
        for i, piece in enumerate(pieces[:4] if n < half else pieces[4:]):
            to = w_buf.at[n, pl.ds(LOCAL + i * PIECE, PIECE)]
            loads.append(pltpu.make_async_copy(piece.at[:, there], to, load_sems.at[n, 2 + i]))
        return loads

    def store_of(n):
        return pltpu.make_async_copy(o_buf.at[n], o_ref.at[0, :, columns_of(n)], store_sems.at[n])

    for n in range(CHUNKS):
        for load in loads_of(n):
            load.start()
    a_buf[:, :LOCAL] = y_ref[:, :LOCAL]
    for i in range(4):
        quarter = lax.bitwise_xor(mine, i)
        to = slice(LOCAL + i * PIECE, LOCAL + (i + 1) * PIECE)

        @pl.when(quarter < 2)
        def _():
            a_buf[:, to] = x_ref[:HALF, pl.ds(pl.multiple_of(quarter * PIECE, PIECE), PIECE)]

        @pl.when(quarter >= 2)
        def _():
            a_buf[:, to] = y_ref[:, pl.ds(pl.multiple_of(quarter * PIECE, PIECE), PIECE)]

    for n in range(CHUNKS):
        for load in loads_of(n):
            load.wait()
        total = acc_buf[n].astype(jnp.float32) + dot_nn(a_buf[...], w_buf[n])
        o_buf[n] = total.astype(jnp.bfloat16)
        store_of(n).start()
    for n in range(CHUNKS):
        store_of(n).wait()


def project(place, row_other, joined, acc, w_own, pieces):
    depth = LOCAL + 4 * PIECE
    return pl.pallas_call(
        project_kernel,
        in_specs=[
            pl.BlockSpec(memory_space=pltpu.SMEM),
            WHOLE,
            WHOLE,
            *[ANYWHERE] * 10,
        ],
        out_specs=ANYWHERE,
        out_shape=pltpu.HBM((1, HALF, WIDTH), jnp.bfloat16),
        scratch_shapes=[
            pltpu.VMEM((HALF, depth), jnp.bfloat16),
            pltpu.VMEM((CHUNKS, depth, CHUNK), jnp.bfloat16),
            pltpu.VMEM((CHUNKS, HALF, CHUNK), jnp.bfloat16),
            pltpu.VMEM((CHUNKS, HALF, CHUNK), jnp.bfloat16),
            pltpu.SemaphoreType.DMA((CHUNKS, 6)),
            pltpu.SemaphoreType.DMA((CHUNKS,)),
        ],
        compiler_params=pltpu.CompilerParams(vmem_limit_bytes=40 << 20),
        cost_estimate=COST,
        name="project",
    )(place, row_other, joined, in_hbm(acc), in_hbm(w_own), *map(in_hbm, pieces))


def slice_kernel(opposite, s_ref, w_ref, x_ref, buf, in_sems, out_sems):
    columns = pl.ds(pl.multiple_of(s_ref[0] * HALF_WIDTH, HALF_WIDTH), HALF_WIDTH)
    quarter = 2 * s_ref[1] + s_ref[2]
    if opposite:
        quarter = 3 - quarter
    loads, stores = [], []
    step = PIECE // SLICE_STEPS
    for n in range(SLICE_STEPS):
        start = pl.multiple_of(quarter * PIECE + n * step, step)
        at = pl.ds(n * step, step)
        loads.append(
            pltpu.make_async_copy(w_ref.at[pl.ds(start, step), columns], buf.at[at], in_sems.at[n])
        )
        stores.append(pltpu.make_async_copy(buf.at[at], x_ref.at[at], out_sems.at[n]))
    for load in loads:
        load.start()
    for load, store in zip(loads, stores):
        load.wait()
        store.start()
    for store in stores:
        store.wait()


SLICE_STEPS = 4


def slice_of(place, w_out, opposite):
    return pl.pallas_call(
        functools.partial(slice_kernel, opposite),
        in_specs=[pl.BlockSpec(memory_space=pltpu.SMEM), pl.BlockSpec(memory_space=pl.ANY)],
        out_specs=pl.BlockSpec(memory_space=pl.ANY),
        out_shape=pltpu.HBM((PIECE, HALF_WIDTH), jnp.bfloat16),
        scratch_shapes=[
            pltpu.VMEM((PIECE, HALF_WIDTH), jnp.bfloat16),
            pltpu.SemaphoreType.DMA((SLICE_STEPS,)),
            pltpu.SemaphoreType.DMA((SLICE_STEPS,)),
        ],
        compiler_params=pltpu.CompilerParams(vmem_limit_bytes=SMALL_VMEM),
        cost_estimate=COST,
        name="slice",
    )(place, in_hbm(w_out))


PACK_STEPS = 4


def pack_kernel(q_ref, k_ref, v_ref, o_ref, buf, in_sems, out_sems):
    step = ROWS // PACK_STEPS
    loads, stores = [], []
    for n in range(PACK_STEPS):
        at = pl.ds(n * step, step)
        loads.append(
            [
                pltpu.make_async_copy(
                    ref.at[0, half, at, :, pl.ds(LOCAL, LOCAL)],
                    buf.at[at, 2 * t + half],
                    in_sems.at[n, 2 * t + half],
                )
                for t, ref in enumerate((q_ref, k_ref, v_ref))
                for half in range(2)
            ]
        )
        stores.append(pltpu.make_async_copy(buf.at[at], o_ref.at[at], out_sems.at[n]))
    for group in loads:
        for load in group:
            load.start()
    for group, store in zip(loads, stores):
        for load in group:
            load.wait()
        store.start()
    for store in stores:
        store.wait()


def packed(*tensors):
    return pl.pallas_call(
        pack_kernel,
        in_specs=[pl.BlockSpec(memory_space=pl.ANY)] * 3,
        out_specs=pl.BlockSpec(memory_space=pl.ANY),
        out_shape=pltpu.HBM((ROWS, 6, 8, LOCAL), jnp.bfloat16),
        scratch_shapes=[
            pltpu.VMEM((ROWS, 6, 8, LOCAL), jnp.bfloat16),
            pltpu.SemaphoreType.DMA((PACK_STEPS, 6)),
            pltpu.SemaphoreType.DMA((PACK_STEPS,)),
        ],
        compiler_params=pltpu.CompilerParams(vmem_limit_bytes=SMALL_VMEM),
        cost_estimate=COST,
        name="pack",
    )(*[in_hbm(t.reshape(1, 2, ROWS, 8, 2 * LOCAL)) for t in tensors]).reshape(ROWS, 3 * COLS, LOCAL)


def on_device(queries, keys, values, w_out):
    place = jnp.stack([*position(), lax.axis_index("head")])
    piece, *col_qkv = lax.optimization_barrier(
        (slice_of(place, w_out, False), queries, keys, values)
    )
    mine = permute(piece, ALONG_X)
    sent = packed(*col_qkv)
    arrived = lax.all_to_all(sent, "ctx", split_axis=0, concat_axis=0, tiled=True)
    mine, w_late, *row_qkv = lax.optimization_barrier((mine, w_out, queries, keys, values))
    away = slice_of(place, w_late, True)
    row_own, row_away = row_attention(*row_qkv)
    acc = project_own_rows(row_own, w_out)
    mine, away, row_away, acc = lax.optimization_barrier((mine, away, row_away, acc))
    near = [mine, permute(mine, ALONG_Z), permute(mine, ALONG_Y), permute(away, ALONG_N)]
    row_other = permute(row_away, TO_HEAD)
    col = column_attention(arrived)
    near, row_other, _ = lax.optimization_barrier((near, row_other, col))
    far = [permute(piece, TO_CORE) for piece in near]
    col = col.reshape(2 * ROWS, 8, LOCAL)
    col = lax.all_to_all(col, ("ctx", "head"), split_axis=0, concat_axis=0, tiled=True)
    joined = join(place, col.reshape(ROWS, 2, 8, LOCAL))
    return project(place, row_other, joined, acc, w_out, near + far)


def solution(mesh):
    return jax.shard_map(
        on_device,
        mesh=mesh,
        in_specs=(
            P("ctx", None, "head"),
            P("ctx", None, "head"),
            P("ctx", None, "head"),
            P("head", None),
        ),
        out_specs=P("ctx", "head", None),
        check_vma=False,
    )
```

```python
import functools
import itertools
import math

import jax
import jax.numpy as jnp
from jax import lax
from jax.experimental import pallas as pl
from jax.experimental.pallas import tpu as pltpu
from jax.sharding import PartitionSpec as P

HD = 128
GROUP = 4
LOCAL = GROUP * HD
LENGTH = 1024
ROWS = 64
HALF = LENGTH // 2
WIDTH = 4096
BLOCK = 256
SCALE = math.log2(math.e) / math.sqrt(HD)
MASKED = -1e30
SMALL_VMEM = 16 << 20
COST = pl.CostEstimate(flops=1 << 20, transcendentals=0, bytes_accessed=1 << 10)
LONG = pl.CostEstimate(flops=1 << 38, transcendentals=0, bytes_accessed=1 << 20)

PLACES = list(itertools.product(range(4), range(4), range(4), range(2)))
HALF_WIDTH = WIDTH // 2
PIECE = LENGTH // 4


def index_of(x, y, z, core):
    return (((z % 4) * 2 + (x % 4) // 2) * 4 + y % 4) * 4 + core * 2 + x % 2


def pair(at, core):
    return at + 1 if at % 2 == core else at - 1


def moves(step):
    return [(index_of(*place), index_of(*step(*place))) for place in PLACES]


ALONG_X = moves(lambda x, y, z, core: (x + 1 - 2 * core, y, z, core))
ALONG_Y = moves(lambda x, y, z, core: (x, pair(y, core), z, core))
ALONG_Z = moves(lambda x, y, z, core: (x, y, pair(z, core), core))
ALONG_N = moves(lambda x, y, z, core: (x - 1 + 2 * (x % 2), y, z, core))
TO_CORE = moves(lambda x, y, z, core: (x, y, z, 1 - core))
TO_HEAD = moves(lambda x, y, z, core: (x + 1 - 2 * (x % 2), y, z, core))


def position():
    ctx = lax.axis_index("ctx")
    return ctx & 1, (ctx >> 1) & 1, (ctx >> 4) & 1


def permute(x, pairs):
    return lax.ppermute(x, ("ctx", "head"), pairs)


def in_hbm(x):
    return pltpu.with_memory_space_constraint(x, pltpu.HBM)


def softmax_rows(scores):
    top = jnp.max(scores, axis=-1, keepdims=True)
    expo = jnp.exp2((scores - top) * SCALE)
    total = jnp.sum(expo, axis=-1, keepdims=True)
    return expo.astype(jnp.bfloat16), total


def dot_nt(a, b):
    return lax.dot_general(a, b, (((1,), (1,)), ((), ())), preferred_element_type=jnp.float32)


def dot_nn(a, b):
    return jnp.dot(a, b, preferred_element_type=jnp.float32)


def row_kernel(q_ref, k_ref, v_ref, own_ref, other_ref):
    me = lax.axis_index("head")
    lower = lax.broadcasted_iota(jnp.int32, (BLOCK, BLOCK), 1) <= lax.broadcasted_iota(
        jnp.int32, (BLOCK, BLOCK), 0
    )
    per_half = HALF // BLOCK
    other_ref[HALF:] = jnp.zeros((HALF, HD), jnp.bfloat16)
    for i in range(LENGTH // BLOCK):
        q = q_ref[0, i * BLOCK : (i + 1) * BLOCK, :]
        end = (i + 1) * BLOCK
        diag = jnp.where(lower, dot_nt(q, k_ref[0, i * BLOCK : end, :]), MASKED)
        if i:
            scores = jnp.concatenate([dot_nt(q, k_ref[0, : i * BLOCK, :]), diag], axis=1)
        else:
            scores = diag
        probs, total = softmax_rows(scores)
        out = (dot_nn(probs, v_ref[0, :end, :]) / total).astype(jnp.bfloat16)
        at = pl.ds((i % per_half) * BLOCK, BLOCK)

        @pl.when(me == i // per_half)
        def _():
            own_ref[at, :] = out

        @pl.when(me != i // per_half)
        def _():
            other_ref[at, :] = out


def row_attention(queries, keys, values):
    spec = pl.BlockSpec((1, LENGTH, HD), lambda h: (0, 0, h))
    return pl.pallas_call(
        row_kernel,
        grid=(GROUP,),
        in_specs=[spec] * 3,
        out_specs=[
            pl.BlockSpec((HALF, HD), lambda h: (0, h)),
            pl.BlockSpec((2 * HALF, HD), lambda h: (0, h)),
        ],
        out_shape=[
            pltpu.HBM((HALF, LOCAL), jnp.bfloat16),
            pltpu.HBM((2 * HALF, LOCAL), jnp.bfloat16),
        ],
        compiler_params=pltpu.CompilerParams(vmem_limit_bytes=SMALL_VMEM),
        cost_estimate=LONG,
        name="row_attention",
    )(in_hbm(queries), in_hbm(keys), in_hbm(values))


COLS = 16
SUB = 16
TOKENS = SUB * COLS
AT_ONCE = 2


def column_kernel(x_ref, o_ref):
    to = lax.broadcasted_iota(jnp.int32, (TOKENS, TOKENS), 0)
    of = lax.broadcasted_iota(jnp.int32, (TOKENS, TOKENS), 1)
    swap = ((to % SUB) * COLS + to // SUB == of).astype(jnp.bfloat16)
    back = ((to % COLS) * SUB + to // COLS == of).astype(jnp.bfloat16)
    blocks = ROWS // SUB
    heads = o_ref.shape[2] // HD
    width = heads * HD
    regrouped = []
    for b in range(blocks):
        x = x_ref[b * SUB : (b + 1) * SUB]
        parts = [x[:, t * COLS : (t + 1) * COLS, :].reshape(TOKENS, width) for t in range(3)]
        regrouped.append(dot_nn(swap, jnp.concatenate(parts, axis=1)).astype(jnp.bfloat16))
    span = TOKENS // blocks
    row_of = (to // span) * SUB + to % SUB
    row_at = (of // span) * SUB + of % SUB
    allowed = ((to // SUB) % (span // SUB) == (of // SUB) % (span // SUB)) & (row_at <= row_of)
    outs = []
    for g in range(TOKENS // span):
        mine = jnp.concatenate([y[g * span : (g + 1) * span] for y in regrouped], axis=0)
        across = []
        for h in range(heads):
            q, k, v = (mine[:, t * width + h * HD : t * width + (h + 1) * HD] for t in range(3))
            probs, total = softmax_rows(jnp.where(allowed, dot_nt(q, k), MASKED))
            across.append((dot_nn(probs, v) / total).astype(jnp.bfloat16))
        outs.append(jnp.concatenate(across, axis=1))
    for b in range(blocks):
        y = jnp.concatenate([o[b * span : (b + 1) * span] for o in outs], axis=0)
        z = dot_nn(back, y).astype(jnp.bfloat16)
        o_ref[b * SUB : (b + 1) * SUB] = z.reshape(SUB, COLS, width)


def column_attention(x):
    return pl.pallas_call(
        column_kernel,
        grid=(GROUP // AT_ONCE,),
        in_specs=[pl.BlockSpec((ROWS, 3 * COLS, AT_ONCE * HD), lambda h: (0, 0, h))],
        out_specs=pl.BlockSpec((ROWS, COLS, AT_ONCE * HD), lambda h: (0, 0, h)),
        out_shape=pltpu.HBM((ROWS, COLS, LOCAL), jnp.bfloat16),
        compiler_params=pltpu.CompilerParams(vmem_limit_bytes=SMALL_VMEM),
        cost_estimate=COST,
        name="column_attention",
    )(x)


TILE = 1024
TILES = WIDTH // TILE
CHUNK = 512
CHUNKS = WIDTH // CHUNK
WHOLE = pl.BlockSpec(memory_space=pltpu.VMEM)
ANYWHERE = pl.BlockSpec(memory_space=pl.ANY)


def own_rows_kernel(a_ref, w_ref, o_ref):
    o_ref[...] = dot_nn(a_ref[...], w_ref[...]).astype(jnp.bfloat16)


def project_own_rows(own, w_own):
    return pl.pallas_call(
        own_rows_kernel,
        grid=(TILES,),
        in_specs=[
            pl.BlockSpec((HALF, LOCAL), lambda n: (0, 0)),
            pl.BlockSpec((LOCAL, TILE), lambda n: (0, n)),
        ],
        out_specs=pl.BlockSpec((HALF, TILE), lambda n: (0, n)),
        out_shape=pltpu.HBM((HALF, WIDTH), jnp.bfloat16),
        compiler_params=pltpu.CompilerParams(vmem_limit_bytes=SMALL_VMEM),
        cost_estimate=COST,
        name="own_rows",
    )(in_hbm(own), in_hbm(w_own))


def head_of(s_ref, i):
    head = lax.bitwise_xor(2 * s_ref[1] + s_ref[2], i)
    return pl.ds(pl.multiple_of(head * HD, HD), HD)


def other_rows_kernel(s_ref, a_ref, acc_ref, *refs):
    pieces, o_ref, join_ref = refs[:4], refs[4], refs[5]

    @pl.when(pl.program_id(0) == 0)
    def _():
        for i in range(4):
            join_ref[:, i * HD : (i + 1) * HD] = a_ref[:, head_of(s_ref, i)]

    weights = jnp.concatenate([piece[...] for piece in pieces], axis=0)
    total = acc_ref[...].astype(jnp.float32) + dot_nn(join_ref[...], weights)
    o_ref[...] = total.astype(jnp.bfloat16)


def project_other_rows(place, other, acc, pieces):
    half = TILES // 2
    return pl.pallas_call(
        other_rows_kernel,
        grid_spec=pltpu.PrefetchScalarGridSpec(
            num_scalar_prefetch=1,
            grid=(half,),
            in_specs=[
                pl.BlockSpec((HALF, LOCAL), lambda n, s: (0, 0)),
                pl.BlockSpec((HALF, TILE), lambda n, s: (0, n + s[0] * half)),
                *[pl.BlockSpec((HD, TILE), lambda n, s: (0, n))] * 4,
            ],
            out_specs=pl.BlockSpec((HALF, TILE), lambda n, s: (0, n)),
            scratch_shapes=[pltpu.VMEM((HALF, LOCAL), jnp.bfloat16)],
        ),
        out_shape=pltpu.HBM((HALF, HALF_WIDTH), jnp.bfloat16),
        compiler_params=pltpu.CompilerParams(vmem_limit_bytes=SMALL_VMEM),
        cost_estimate=COST,
        name="other_rows",
    )(place, in_hbm(other), in_hbm(acc), *map(in_hbm, pieces))


def join_kernel(s_ref, x_ref, a_ref):
    me = s_ref[3]
    a_ref[:, :LOCAL] = x_ref[:, me].reshape(HALF, LOCAL)
    for i in range(4):
        other = x_ref[:, 1 - me, :, head_of(s_ref, i)].reshape(HALF, HD)
        a_ref[:, LOCAL + i * HD : LOCAL + (i + 1) * HD] = other


def join(place, attended):
    return pl.pallas_call(
        join_kernel,
        in_specs=[pl.BlockSpec(memory_space=pltpu.SMEM), WHOLE],
        out_specs=WHOLE,
        out_shape=jax.ShapeDtypeStruct((HALF, 2 * LOCAL), jnp.bfloat16),
        compiler_params=pltpu.CompilerParams(vmem_limit_bytes=SMALL_VMEM),
        cost_estimate=LONG,
        name="join",
    )(place, attended)


def project_kernel(s_ref, x_ref, y_ref, near_ref, far_ref, w_ref, *refs):
    pieces, o_ref = refs[:8], refs[8]
    a_buf, w_buf, acc_buf, o_buf, load_sems, store_sems, row_sems = refs[9:]
    half = CHUNKS // 2
    depth = 2 * LOCAL

    def columns_of(n):
        at = lax.rem(n + s_ref[0] * half, CHUNKS)
        return pl.ds(pl.multiple_of(at * CHUNK, CHUNK), CHUNK)

    def loads_of(n):
        columns = columns_of(n)
        there = pl.ds(n % half * CHUNK, CHUNK)
        sems = load_sems.at[n]
        acc = near_ref.at[:, there] if n < half else far_ref.at[:, columns]
        copies = [
            (acc, acc_buf.at[n]),
            (w_ref.at[pl.ds(LOCAL, LOCAL), columns], w_buf.at[n, pl.ds(0, LOCAL)]),
        ]
        for i, piece in enumerate(pieces[:4] if n < half else pieces[4:]):
            to = w_buf.at[n, pl.ds(LOCAL + i * HD, HD)]
            copies.append((piece.at[pl.ds(HD, HD), there], to))
            if n >= half:
                to = w_buf.at[n, pl.ds(depth + i * HD, HD)]
                copies.append((piece.at[pl.ds(0, HD), there], to))
        return [pltpu.make_async_copy(*copy, sems.at[i]) for i, copy in enumerate(copies)]

    def store_of(n):
        return pltpu.make_async_copy(o_buf.at[n], o_ref.at[0, :, columns_of(n)], store_sems.at[n])

    for n in range(CHUNKS):
        for load in loads_of(n):
            load.start()
    rows = [
        pltpu.make_async_copy(
            x_ref.at[pl.ds(0, HALF), head_of(s_ref, i)],
            a_buf.at[:, pl.ds(i * HD, HD)],
            row_sems.at[i],
        )
        for i in range(4)
    ]
    for load in rows:
        load.start()
    for n in range(CHUNKS):
        for load in loads_of(n) + (rows if n == half else []):
            load.wait()
        total = acc_buf[n].astype(jnp.float32) + dot_nn(y_ref[...], w_buf[n, :depth])
        if n >= half:
            total += dot_nn(a_buf[...], w_buf[n, depth:])
        o_buf[n] = total.astype(jnp.bfloat16)
        store_of(n).start()
    for n in range(CHUNKS):
        store_of(n).wait()


def project(place, row_other, joined, acc_near, acc, w_own, pieces):
    return pl.pallas_call(
        project_kernel,
        in_specs=[
            pl.BlockSpec(memory_space=pltpu.SMEM),
            ANYWHERE,
            WHOLE,
            *[ANYWHERE] * 11,
        ],
        out_specs=ANYWHERE,
        out_shape=pltpu.HBM((1, HALF, WIDTH), jnp.bfloat16),
        scratch_shapes=[
            pltpu.VMEM((HALF, LOCAL), jnp.bfloat16),
            pltpu.VMEM((CHUNKS, 3 * LOCAL, CHUNK), jnp.bfloat16),
            pltpu.VMEM((CHUNKS, HALF, CHUNK), jnp.bfloat16),
            pltpu.VMEM((CHUNKS, HALF, CHUNK), jnp.bfloat16),
            pltpu.SemaphoreType.DMA((CHUNKS, 10)),
            pltpu.SemaphoreType.DMA((CHUNKS,)),
            pltpu.SemaphoreType.DMA((4,)),
        ],
        compiler_params=pltpu.CompilerParams(vmem_limit_bytes=40 << 20),
        cost_estimate=COST,
        name="project",
    )(place, in_hbm(row_other), joined, *map(in_hbm, (acc_near, acc, w_own, *pieces)))


def slice_kernel(opposite, s_ref, w_ref, x_ref, buf, in_sems, out_sems):
    columns = pl.ds(pl.multiple_of(s_ref[0] * HALF_WIDTH, HALF_WIDTH), HALF_WIDTH)
    head = 2 * s_ref[1] + s_ref[2]
    if opposite:
        head = 3 - head
    loads, stores = [], []
    step = PIECE // SLICE_STEPS
    each = SLICE_STEPS // 2
    for n in range(SLICE_STEPS):
        start = pl.multiple_of(n // each * LOCAL + head * HD + n % each * step, step)
        at = pl.ds(n * step, step)
        loads.append(
            pltpu.make_async_copy(w_ref.at[pl.ds(start, step), columns], buf.at[at], in_sems.at[n])
        )
        stores.append(pltpu.make_async_copy(buf.at[at], x_ref.at[at], out_sems.at[n]))
    for load in loads:
        load.start()
    for load, store in zip(loads, stores):
        load.wait()
        store.start()
    for store in stores:
        store.wait()


SLICE_STEPS = 4


def slice_of(place, w_out, opposite):
    return pl.pallas_call(
        functools.partial(slice_kernel, opposite),
        in_specs=[pl.BlockSpec(memory_space=pltpu.SMEM), pl.BlockSpec(memory_space=pl.ANY)],
        out_specs=pl.BlockSpec(memory_space=pl.ANY),
        out_shape=pltpu.HBM((PIECE, HALF_WIDTH), jnp.bfloat16),
        scratch_shapes=[
            pltpu.VMEM((PIECE, HALF_WIDTH), jnp.bfloat16),
            pltpu.SemaphoreType.DMA((SLICE_STEPS,)),
            pltpu.SemaphoreType.DMA((SLICE_STEPS,)),
        ],
        compiler_params=pltpu.CompilerParams(vmem_limit_bytes=SMALL_VMEM),
        cost_estimate=COST,
        name="slice",
    )(place, in_hbm(w_out))


PACK_STEPS = 4


def pack_kernel(q_ref, k_ref, v_ref, o_ref, buf, in_sems, out_sems):
    step = ROWS // PACK_STEPS
    loads, stores = [], []
    for n in range(PACK_STEPS):
        at = pl.ds(n * step, step)
        loads.append(
            [
                pltpu.make_async_copy(
                    ref.at[0, half, at, :, pl.ds(LOCAL, LOCAL)],
                    buf.at[at, 2 * t + half],
                    in_sems.at[n, 2 * t + half],
                )
                for t, ref in enumerate((q_ref, k_ref, v_ref))
                for half in range(2)
            ]
        )
        stores.append(pltpu.make_async_copy(buf.at[at], o_ref.at[at], out_sems.at[n]))
    for group in loads:
        for load in group:
            load.start()
    for group, store in zip(loads, stores):
        for load in group:
            load.wait()
        store.start()
    for store in stores:
        store.wait()


def packed(*tensors):
    return pl.pallas_call(
        pack_kernel,
        in_specs=[pl.BlockSpec(memory_space=pl.ANY)] * 3,
        out_specs=pl.BlockSpec(memory_space=pl.ANY),
        out_shape=pltpu.HBM((ROWS, 6, 8, LOCAL), jnp.bfloat16),
        scratch_shapes=[
            pltpu.VMEM((ROWS, 6, 8, LOCAL), jnp.bfloat16),
            pltpu.SemaphoreType.DMA((PACK_STEPS, 6)),
            pltpu.SemaphoreType.DMA((PACK_STEPS,)),
        ],
        compiler_params=pltpu.CompilerParams(vmem_limit_bytes=SMALL_VMEM),
        cost_estimate=COST,
        name="pack",
    )(*[in_hbm(t.reshape(1, 2, ROWS, 8, 2 * LOCAL)) for t in tensors]).reshape(ROWS, 3 * COLS, LOCAL)


def on_device(queries, keys, values, w_out):
    place = jnp.stack([*position(), lax.axis_index("head")])
    piece, *col_qkv = lax.optimization_barrier(
        (slice_of(place, w_out, False), queries, keys, values)
    )
    mine = permute(piece, ALONG_X)
    sent = packed(*col_qkv)
    arrived = lax.all_to_all(sent, "ctx", split_axis=0, concat_axis=0, tiled=True)
    mine, w_late, *row_qkv = lax.optimization_barrier((mine, w_out, queries, keys, values))
    away = slice_of(place, w_late, True)
    row_own, row_away = row_attention(*row_qkv)
    acc = project_own_rows(row_own, w_out)
    mine, away, row_away, acc = lax.optimization_barrier((mine, away, row_away, acc))
    near = [mine, permute(mine, ALONG_Z), permute(mine, ALONG_Y), permute(away, ALONG_N)]
    row_other = permute(row_away, TO_HEAD)
    col = column_attention(arrived)
    near, row_other, _ = lax.optimization_barrier((near, row_other, col))
    far = [permute(piece, TO_CORE) for piece in near]
    col = col.reshape(2 * ROWS, 8, LOCAL)
    col = lax.all_to_all(col, ("ctx", "head"), split_axis=0, concat_axis=0, tiled=True)
    acc_near = project_other_rows(place, row_other, acc, near)
    col, acc_near = lax.optimization_barrier((col, acc_near))
    joined = join(place, col.reshape(ROWS, 2, 8, LOCAL))
    return project(place, row_other, joined, acc_near, acc, w_out, near + far)


def solution(mesh):
    return jax.shard_map(
        on_device,
        mesh=mesh,
        in_specs=(
            P("ctx", None, "head"),
            P("ctx", None, "head"),
            P("ctx", None, "head"),
            P("head", None),
        ),
        out_specs=P("ctx", "head", None),
        check_vma=False,
    )
```

```python
import functools
import itertools
import math

import jax
import jax.numpy as jnp
from jax import lax
from jax.experimental import pallas as pl
from jax.experimental.pallas import tpu as pltpu
from jax.sharding import PartitionSpec as P

HD = 128
GROUP = 4
LOCAL = GROUP * HD
LENGTH = 1024
ROWS = 64
HALF = LENGTH // 2
WIDTH = 4096
BLOCK = 256
SCALE = math.log2(math.e) / math.sqrt(HD)
MASKED = -1e30
SMALL_VMEM = 16 << 20
COST = pl.CostEstimate(flops=1 << 20, transcendentals=0, bytes_accessed=1 << 10)
LONG = pl.CostEstimate(flops=1 << 38, transcendentals=0, bytes_accessed=1 << 20)

PLACES = list(itertools.product(range(4), range(4), range(4), range(2)))
HALF_WIDTH = WIDTH // 2
PIECE = LENGTH // 4


def index_of(x, y, z, core):
    return (((z % 4) * 2 + (x % 4) // 2) * 4 + y % 4) * 4 + core * 2 + x % 2


def pair(at, core):
    return at + 1 if at % 2 == core else at - 1


def moves(step):
    return [(index_of(*place), index_of(*step(*place))) for place in PLACES]


ALONG_X = moves(lambda x, y, z, core: (x + 1 - 2 * core, y, z, core))
ALONG_Y = moves(lambda x, y, z, core: (x, pair(y, core), z, core))
ALONG_Z = moves(lambda x, y, z, core: (x, y, pair(z, core), core))
ALONG_N = moves(lambda x, y, z, core: (x - 1 + 2 * (x % 2), y, z, core))
TO_CORE = moves(lambda x, y, z, core: (x, y, z, 1 - core))
TO_HEAD = moves(lambda x, y, z, core: (x + 1 - 2 * (x % 2), y, z, core))


def position():
    ctx = lax.axis_index("ctx")
    return ctx & 1, (ctx >> 1) & 1, (ctx >> 4) & 1


def permute(x, pairs):
    return lax.ppermute(x, ("ctx", "head"), pairs)


def in_hbm(x):
    return pltpu.with_memory_space_constraint(x, pltpu.HBM)


def softmax_rows(scores):
    top = jnp.max(scores, axis=-1, keepdims=True)
    expo = jnp.exp2((scores - top) * SCALE)
    total = jnp.sum(expo, axis=-1, keepdims=True)
    return expo.astype(jnp.bfloat16), total


def dot_nt(a, b):
    return lax.dot_general(a, b, (((1,), (1,)), ((), ())), preferred_element_type=jnp.float32)


def dot_nn(a, b):
    return jnp.dot(a, b, preferred_element_type=jnp.float32)


def row_kernel(q_ref, k_ref, v_ref, own_ref, other_ref):
    me = lax.axis_index("head")
    lower = lax.broadcasted_iota(jnp.int32, (BLOCK, BLOCK), 1) <= lax.broadcasted_iota(
        jnp.int32, (BLOCK, BLOCK), 0
    )
    per_half = HALF // BLOCK
    other_ref[HALF:] = jnp.zeros((HALF, HD), jnp.bfloat16)
    for i in range(LENGTH // BLOCK):
        q = q_ref[0, i * BLOCK : (i + 1) * BLOCK, :]
        end = (i + 1) * BLOCK
        diag = jnp.where(lower, dot_nt(q, k_ref[0, i * BLOCK : end, :]), MASKED)
        if i:
            scores = jnp.concatenate([dot_nt(q, k_ref[0, : i * BLOCK, :]), diag], axis=1)
        else:
            scores = diag
        probs, total = softmax_rows(scores)
        out = (dot_nn(probs, v_ref[0, :end, :]) / total).astype(jnp.bfloat16)
        at = pl.ds((i % per_half) * BLOCK, BLOCK)

        @pl.when(me == i // per_half)
        def _():
            own_ref[at, :] = out

        @pl.when(me != i // per_half)
        def _():
            other_ref[at, :] = out


def row_attention(queries, keys, values):
    spec = pl.BlockSpec((1, LENGTH, HD), lambda h: (0, 0, h))
    return pl.pallas_call(
        row_kernel,
        grid=(GROUP,),
        in_specs=[spec] * 3,
        out_specs=[
            pl.BlockSpec((HALF, HD), lambda h: (0, h)),
            pl.BlockSpec((2 * HALF, HD), lambda h: (0, h)),
        ],
        out_shape=[
            pltpu.HBM((HALF, LOCAL), jnp.bfloat16),
            pltpu.HBM((2 * HALF, LOCAL), jnp.bfloat16),
        ],
        compiler_params=pltpu.CompilerParams(vmem_limit_bytes=SMALL_VMEM),
        cost_estimate=LONG,
        name="row_attention",
    )(in_hbm(queries), in_hbm(keys), in_hbm(values))


COLS = 16
SUB = 16
TOKENS = SUB * COLS
AT_ONCE = 2


def column_kernel(x_ref, o_ref):
    to = lax.broadcasted_iota(jnp.int32, (TOKENS, TOKENS), 0)
    of = lax.broadcasted_iota(jnp.int32, (TOKENS, TOKENS), 1)
    swap = ((to % SUB) * COLS + to // SUB == of).astype(jnp.bfloat16)
    back = ((to % COLS) * SUB + to // COLS == of).astype(jnp.bfloat16)
    blocks = ROWS // SUB
    heads = o_ref.shape[2] // HD
    width = heads * HD
    regrouped = []
    for b in range(blocks):
        x = x_ref[b * SUB : (b + 1) * SUB]
        parts = [x[:, t * COLS : (t + 1) * COLS, :].reshape(TOKENS, width) for t in range(3)]
        regrouped.append(dot_nn(swap, jnp.concatenate(parts, axis=1)).astype(jnp.bfloat16))
    span = TOKENS // blocks
    row_of = (to // span) * SUB + to % SUB
    row_at = (of // span) * SUB + of % SUB
    allowed = ((to // SUB) % (span // SUB) == (of // SUB) % (span // SUB)) & (row_at <= row_of)
    outs = []
    for g in range(TOKENS // span):
        mine = jnp.concatenate([y[g * span : (g + 1) * span] for y in regrouped], axis=0)
        across = []
        for h in range(heads):
            q, k, v = (mine[:, t * width + h * HD : t * width + (h + 1) * HD] for t in range(3))
            probs, total = softmax_rows(jnp.where(allowed, dot_nt(q, k), MASKED))
            across.append((dot_nn(probs, v) / total).astype(jnp.bfloat16))
        outs.append(jnp.concatenate(across, axis=1))
    for b in range(blocks):
        y = jnp.concatenate([o[b * span : (b + 1) * span] for o in outs], axis=0)
        z = dot_nn(back, y).astype(jnp.bfloat16)
        o_ref[b * SUB : (b + 1) * SUB] = z.reshape(SUB, COLS, width)


def column_attention(x):
    return pl.pallas_call(
        column_kernel,
        grid=(GROUP // AT_ONCE,),
        in_specs=[pl.BlockSpec((ROWS, 3 * COLS, AT_ONCE * HD), lambda h: (0, 0, h))],
        out_specs=pl.BlockSpec((ROWS, COLS, AT_ONCE * HD), lambda h: (0, 0, h)),
        out_shape=pltpu.HBM((ROWS, COLS, LOCAL), jnp.bfloat16),
        compiler_params=pltpu.CompilerParams(vmem_limit_bytes=SMALL_VMEM),
        cost_estimate=COST,
        name="column_attention",
    )(x)


TILE = 1024
TILES = WIDTH // TILE
CHUNK = 512
CHUNKS = WIDTH // CHUNK
WHOLE = pl.BlockSpec(memory_space=pltpu.VMEM)
ANYWHERE = pl.BlockSpec(memory_space=pl.ANY)


def own_rows_kernel(a_ref, w_ref, o_ref):
    o_ref[...] = dot_nn(a_ref[...], w_ref[...]).astype(jnp.bfloat16)


def project_own_rows(own, w_own):
    return pl.pallas_call(
        own_rows_kernel,
        grid=(TILES,),
        in_specs=[
            pl.BlockSpec((HALF, LOCAL), lambda n: (0, 0)),
            pl.BlockSpec((LOCAL, TILE), lambda n: (0, n)),
        ],
        out_specs=pl.BlockSpec((HALF, TILE), lambda n: (0, n)),
        out_shape=pltpu.HBM((HALF, WIDTH), jnp.bfloat16),
        compiler_params=pltpu.CompilerParams(vmem_limit_bytes=SMALL_VMEM),
        cost_estimate=COST,
        name="own_rows",
    )(in_hbm(own), in_hbm(w_own))


def head_of(s_ref, i):
    head = lax.bitwise_xor(2 * s_ref[1] + s_ref[2], i)
    return pl.ds(pl.multiple_of(head * HD, HD), HD)


def other_rows_kernel(s_ref, a_ref, acc_ref, *refs):
    pieces, o_ref, join_ref = refs[:4], refs[4], refs[5]

    @pl.when(pl.program_id(0) == 0)
    def _():
        for i in range(4):
            join_ref[:, i * HD : (i + 1) * HD] = a_ref[:, head_of(s_ref, i)]

    weights = jnp.concatenate([piece[...] for piece in pieces], axis=0)
    total = acc_ref[...].astype(jnp.float32) + dot_nn(join_ref[...], weights)
    o_ref[...] = total.astype(jnp.bfloat16)


def project_other_rows(place, other, acc, pieces):
    half = TILES // 2
    return pl.pallas_call(
        other_rows_kernel,
        grid_spec=pltpu.PrefetchScalarGridSpec(
            num_scalar_prefetch=1,
            grid=(half,),
            in_specs=[
                pl.BlockSpec((HALF, LOCAL), lambda n, s: (0, 0)),
                pl.BlockSpec((HALF, TILE), lambda n, s: (0, n + s[0] * half)),
                *[pl.BlockSpec((HD, TILE), lambda n, s: (0, n))] * 4,
            ],
            out_specs=pl.BlockSpec((HALF, TILE), lambda n, s: (0, n)),
            scratch_shapes=[pltpu.VMEM((HALF, LOCAL), jnp.bfloat16)],
        ),
        out_shape=pltpu.HBM((HALF, HALF_WIDTH), jnp.bfloat16),
        compiler_params=pltpu.CompilerParams(vmem_limit_bytes=SMALL_VMEM),
        cost_estimate=COST,
        name="other_rows",
    )(place, in_hbm(other), in_hbm(acc), *map(in_hbm, pieces))


def join_kernel(s_ref, x_ref, a_ref):
    me = s_ref[3]
    a_ref[:, :LOCAL] = x_ref[:, me].reshape(HALF, LOCAL)
    for i in range(4):
        other = x_ref[:, 1 - me, :, head_of(s_ref, i)].reshape(HALF, HD)
        a_ref[:, LOCAL + i * HD : LOCAL + (i + 1) * HD] = other


def join(place, attended):
    return pl.pallas_call(
        join_kernel,
        in_specs=[pl.BlockSpec(memory_space=pltpu.SMEM), WHOLE],
        out_specs=WHOLE,
        out_shape=jax.ShapeDtypeStruct((HALF, 2 * LOCAL), jnp.bfloat16),
        compiler_params=pltpu.CompilerParams(vmem_limit_bytes=SMALL_VMEM),
        cost_estimate=LONG,
        name="join",
    )(place, attended)


def project_kernel(s_ref, x_ref, y_ref, near_ref, far_ref, w_ref, *refs):
    pieces, o_ref = refs[:8], refs[8]
    a_buf, w_buf, acc_buf, o_buf, load_sems, store_sems, x_buf, row_sem = refs[9:]
    half = CHUNKS // 2
    depth = 2 * LOCAL

    def columns_of(n):
        at = lax.rem(n + s_ref[0] * half, CHUNKS)
        return pl.ds(pl.multiple_of(at * CHUNK, CHUNK), CHUNK)

    def loads_of(n):
        columns = columns_of(n)
        there = pl.ds(n % half * CHUNK, CHUNK)
        sems = load_sems.at[n]
        acc = near_ref.at[:, there] if n < half else far_ref.at[:, columns]
        copies = [
            (acc, acc_buf.at[n]),
            (w_ref.at[pl.ds(LOCAL, LOCAL), columns], w_buf.at[n, pl.ds(0, LOCAL)]),
        ]
        for i, piece in enumerate(pieces[:4] if n < half else pieces[4:]):
            to = w_buf.at[n, pl.ds(LOCAL + i * HD, HD)]
            copies.append((piece.at[pl.ds(HD, HD), there], to))
            if n >= half:
                to = w_buf.at[n, pl.ds(depth + i * HD, HD)]
                copies.append((piece.at[pl.ds(0, HD), there], to))
        return [pltpu.make_async_copy(*copy, sems.at[i]) for i, copy in enumerate(copies)]

    def store_of(n):
        return pltpu.make_async_copy(o_buf.at[n], o_ref.at[0, :, columns_of(n)], store_sems.at[n])

    for n in range(CHUNKS):
        for load in loads_of(n):
            load.start()
    rows = pltpu.make_async_copy(x_ref.at[pl.ds(0, HALF)], x_buf, row_sem)
    rows.start()
    for n in range(CHUNKS):
        for load in loads_of(n):
            load.wait()
        if n == half:
            rows.wait()
            for i in range(4):
                a_buf[:, i * HD : (i + 1) * HD] = x_buf[:, head_of(s_ref, i)]
        total = acc_buf[n].astype(jnp.float32) + dot_nn(y_ref[...], w_buf[n, :depth])
        if n >= half:
            total += dot_nn(a_buf[...], w_buf[n, depth:])
        o_buf[n] = total.astype(jnp.bfloat16)
        store_of(n).start()
    for n in range(CHUNKS):
        store_of(n).wait()


def project(place, row_other, joined, acc_near, acc, w_own, pieces):
    return pl.pallas_call(
        project_kernel,
        in_specs=[
            pl.BlockSpec(memory_space=pltpu.SMEM),
            ANYWHERE,
            WHOLE,
            *[ANYWHERE] * 11,
        ],
        out_specs=ANYWHERE,
        out_shape=pltpu.HBM((1, HALF, WIDTH), jnp.bfloat16),
        scratch_shapes=[
            pltpu.VMEM((HALF, LOCAL), jnp.bfloat16),
            pltpu.VMEM((CHUNKS, 3 * LOCAL, CHUNK), jnp.bfloat16),
            pltpu.VMEM((CHUNKS, HALF, CHUNK), jnp.bfloat16),
            pltpu.VMEM((CHUNKS, HALF, CHUNK), jnp.bfloat16),
            pltpu.SemaphoreType.DMA((CHUNKS, 10)),
            pltpu.SemaphoreType.DMA((CHUNKS,)),
            pltpu.VMEM((HALF, LOCAL), jnp.bfloat16),
            pltpu.SemaphoreType.DMA(()),
        ],
        compiler_params=pltpu.CompilerParams(vmem_limit_bytes=40 << 20),
        cost_estimate=COST,
        name="project",
    )(place, in_hbm(row_other), joined, *map(in_hbm, (acc_near, acc, w_own, *pieces)))


def slice_kernel(opposite, s_ref, w_ref, x_ref, buf, in_sems, out_sems):
    columns = pl.ds(pl.multiple_of(s_ref[0] * HALF_WIDTH, HALF_WIDTH), HALF_WIDTH)
    head = 2 * s_ref[1] + s_ref[2]
    if opposite:
        head = 3 - head
    loads, stores = [], []
    step = PIECE // SLICE_STEPS
    each = SLICE_STEPS // 2
    for n in range(SLICE_STEPS):
        start = pl.multiple_of(n // each * LOCAL + head * HD + n % each * step, step)
        at = pl.ds(n * step, step)
        loads.append(
            pltpu.make_async_copy(w_ref.at[pl.ds(start, step), columns], buf.at[at], in_sems.at[n])
        )
        stores.append(pltpu.make_async_copy(buf.at[at], x_ref.at[at], out_sems.at[n]))
    for load in loads:
        load.start()
    for load, store in zip(loads, stores):
        load.wait()
        store.start()
    for store in stores:
        store.wait()


SLICE_STEPS = 4


def slice_of(place, w_out, opposite):
    return pl.pallas_call(
        functools.partial(slice_kernel, opposite),
        in_specs=[pl.BlockSpec(memory_space=pltpu.SMEM), pl.BlockSpec(memory_space=pl.ANY)],
        out_specs=pl.BlockSpec(memory_space=pl.ANY),
        out_shape=pltpu.HBM((PIECE, HALF_WIDTH), jnp.bfloat16),
        scratch_shapes=[
            pltpu.VMEM((PIECE, HALF_WIDTH), jnp.bfloat16),
            pltpu.SemaphoreType.DMA((SLICE_STEPS,)),
            pltpu.SemaphoreType.DMA((SLICE_STEPS,)),
        ],
        compiler_params=pltpu.CompilerParams(vmem_limit_bytes=SMALL_VMEM),
        cost_estimate=COST,
        name="slice",
    )(place, in_hbm(w_out))


PACK_STEPS = 4


def pack_kernel(q_ref, k_ref, v_ref, o_ref, buf, in_sems, out_sems):
    step = ROWS // PACK_STEPS
    loads, stores = [], []
    for n in range(PACK_STEPS):
        at = pl.ds(n * step, step)
        loads.append(
            [
                pltpu.make_async_copy(
                    ref.at[0, half, at, :, pl.ds(LOCAL, LOCAL)],
                    buf.at[at, 2 * t + half],
                    in_sems.at[n, 2 * t + half],
                )
                for t, ref in enumerate((q_ref, k_ref, v_ref))
                for half in range(2)
            ]
        )
        stores.append(pltpu.make_async_copy(buf.at[at], o_ref.at[at], out_sems.at[n]))
    for group in loads:
        for load in group:
            load.start()
    for group, store in zip(loads, stores):
        for load in group:
            load.wait()
        store.start()
    for store in stores:
        store.wait()


def packed(*tensors):
    return pl.pallas_call(
        pack_kernel,
        in_specs=[pl.BlockSpec(memory_space=pl.ANY)] * 3,
        out_specs=pl.BlockSpec(memory_space=pl.ANY),
        out_shape=pltpu.HBM((ROWS, 6, 8, LOCAL), jnp.bfloat16),
        scratch_shapes=[
            pltpu.VMEM((ROWS, 6, 8, LOCAL), jnp.bfloat16),
            pltpu.SemaphoreType.DMA((PACK_STEPS, 6)),
            pltpu.SemaphoreType.DMA((PACK_STEPS,)),
        ],
        compiler_params=pltpu.CompilerParams(vmem_limit_bytes=SMALL_VMEM),
        cost_estimate=COST,
        name="pack",
    )(*[in_hbm(t.reshape(1, 2, ROWS, 8, 2 * LOCAL)) for t in tensors]).reshape(ROWS, 3 * COLS, LOCAL)


def on_device(queries, keys, values, w_out):
    place = jnp.stack([*position(), lax.axis_index("head")])
    piece, *col_qkv = lax.optimization_barrier(
        (slice_of(place, w_out, False), queries, keys, values)
    )
    mine = permute(piece, ALONG_X)
    sent = packed(*col_qkv)
    arrived = lax.all_to_all(sent, "ctx", split_axis=0, concat_axis=0, tiled=True)
    mine, w_late, *row_qkv = lax.optimization_barrier((mine, w_out, queries, keys, values))
    away = slice_of(place, w_late, True)
    row_own, row_away = row_attention(*row_qkv)
    acc = project_own_rows(row_own, w_out)
    mine, away, row_away, acc = lax.optimization_barrier((mine, away, row_away, acc))
    near = [mine, permute(mine, ALONG_Z), permute(mine, ALONG_Y), permute(away, ALONG_N)]
    row_other = permute(row_away, TO_HEAD)
    col = column_attention(arrived)
    near, row_other, _ = lax.optimization_barrier((near, row_other, col))
    far = [permute(piece, TO_CORE) for piece in near]
    col = col.reshape(2 * ROWS, 8, LOCAL)
    col = lax.all_to_all(col, ("ctx", "head"), split_axis=0, concat_axis=0, tiled=True)
    acc_near = project_other_rows(place, row_other, acc, near)
    col, acc_near = lax.optimization_barrier((col, acc_near))
    joined = join(place, col.reshape(ROWS, 2, 8, LOCAL))
    return project(place, row_other, joined, acc_near, acc, w_out, near + far)


def solution(mesh):
    return jax.shard_map(
        on_device,
        mesh=mesh,
        in_specs=(
            P("ctx", None, "head"),
            P("ctx", None, "head"),
            P("ctx", None, "head"),
            P("head", None),
        ),
        out_specs=P("ctx", "head", None),
        check_vma=False,
    )
```

```python
import functools
import itertools
import math

import jax
import jax.numpy as jnp
from jax import lax
from jax.experimental import pallas as pl
from jax.experimental.pallas import tpu as pltpu
from jax.sharding import PartitionSpec as P

HD = 128
GROUP = 4
LOCAL = GROUP * HD
LENGTH = 1024
ROWS = 64
HALF = LENGTH // 2
WIDTH = 4096
BLOCK = 256
SCALE = math.log2(math.e) / math.sqrt(HD)
MASKED = -1e30
SMALL_VMEM = 16 << 20
COST = pl.CostEstimate(flops=1 << 20, transcendentals=0, bytes_accessed=1 << 10)
LONG = pl.CostEstimate(flops=1 << 38, transcendentals=0, bytes_accessed=1 << 20)

PLACES = list(itertools.product(range(4), range(4), range(4), range(2)))
HALF_WIDTH = WIDTH // 2
PIECE = LENGTH // 4


def index_of(x, y, z, core):
    return (((z % 4) * 2 + (x % 4) // 2) * 4 + y % 4) * 4 + core * 2 + x % 2


def pair(at, core):
    return at + 1 if at % 2 == core else at - 1


def moves(step):
    return [(index_of(*place), index_of(*step(*place))) for place in PLACES]


ALONG_X = moves(lambda x, y, z, core: (x + 1 - 2 * core, y, z, core))
ALONG_Y = moves(lambda x, y, z, core: (x, pair(y, core), z, core))
ALONG_Z = moves(lambda x, y, z, core: (x, y, pair(z, core), core))
ALONG_N = moves(lambda x, y, z, core: (x - 1 + 2 * (x % 2), y, z, core))
TO_CORE = moves(lambda x, y, z, core: (x, y, z, 1 - core))
TO_HEAD = moves(lambda x, y, z, core: (x + 1 - 2 * (x % 2), y, z, core))


def position():
    ctx = lax.axis_index("ctx")
    return ctx & 1, (ctx >> 1) & 1, (ctx >> 4) & 1


def permute(x, pairs):
    return lax.ppermute(x, ("ctx", "head"), pairs)


def in_hbm(x):
    return pltpu.with_memory_space_constraint(x, pltpu.HBM)


def softmax_rows(scores):
    top = jnp.max(scores, axis=-1, keepdims=True)
    expo = jnp.exp2((scores - top) * SCALE)
    total = jnp.sum(expo, axis=-1, keepdims=True)
    return expo.astype(jnp.bfloat16), total


def dot_nt(a, b):
    return lax.dot_general(a, b, (((1,), (1,)), ((), ())), preferred_element_type=jnp.float32)


def dot_nn(a, b):
    return jnp.dot(a, b, preferred_element_type=jnp.float32)


def row_kernel(q_ref, k_ref, v_ref, own_ref, other_ref):
    me = lax.axis_index("head")
    lower = lax.broadcasted_iota(jnp.int32, (BLOCK, BLOCK), 1) <= lax.broadcasted_iota(
        jnp.int32, (BLOCK, BLOCK), 0
    )
    per_half = HALF // BLOCK
    other_ref[HALF:] = jnp.zeros((HALF, HD), jnp.bfloat16)
    for i in range(LENGTH // BLOCK):
        q = q_ref[0, i * BLOCK : (i + 1) * BLOCK, :]
        end = (i + 1) * BLOCK
        diag = jnp.where(lower, dot_nt(q, k_ref[0, i * BLOCK : end, :]), MASKED)
        if i:
            scores = jnp.concatenate([dot_nt(q, k_ref[0, : i * BLOCK, :]), diag], axis=1)
        else:
            scores = diag
        probs, total = softmax_rows(scores)
        out = (dot_nn(probs, v_ref[0, :end, :]) / total).astype(jnp.bfloat16)
        at = pl.ds((i % per_half) * BLOCK, BLOCK)

        @pl.when(me == i // per_half)
        def _():
            own_ref[at, :] = out

        @pl.when(me != i // per_half)
        def _():
            other_ref[at, :] = out


def row_attention(queries, keys, values):
    spec = pl.BlockSpec((1, LENGTH, HD), lambda h: (0, 0, h))
    return pl.pallas_call(
        row_kernel,
        grid=(GROUP,),
        in_specs=[spec] * 3,
        out_specs=[
            pl.BlockSpec((HALF, HD), lambda h: (0, h)),
            pl.BlockSpec((2 * HALF, HD), lambda h: (0, h)),
        ],
        out_shape=[
            pltpu.HBM((HALF, LOCAL), jnp.bfloat16),
            pltpu.HBM((2 * HALF, LOCAL), jnp.bfloat16),
        ],
        compiler_params=pltpu.CompilerParams(vmem_limit_bytes=SMALL_VMEM),
        cost_estimate=LONG,
        name="row_attention",
    )(in_hbm(queries), in_hbm(keys), in_hbm(values))


COLS = 16
SUB = 16
TOKENS = SUB * COLS
AT_ONCE = 2


def column_kernel(x_ref, o_ref):
    to = lax.broadcasted_iota(jnp.int32, (TOKENS, TOKENS), 0)
    of = lax.broadcasted_iota(jnp.int32, (TOKENS, TOKENS), 1)
    swap = ((to % SUB) * COLS + to // SUB == of).astype(jnp.bfloat16)
    back = ((to % COLS) * SUB + to // COLS == of).astype(jnp.bfloat16)
    blocks = ROWS // SUB
    heads = o_ref.shape[2] // HD
    width = heads * HD
    regrouped = []
    for b in range(blocks):
        x = x_ref[b * SUB : (b + 1) * SUB]
        parts = [x[:, t * COLS : (t + 1) * COLS, :].reshape(TOKENS, width) for t in range(3)]
        regrouped.append(dot_nn(swap, jnp.concatenate(parts, axis=1)).astype(jnp.bfloat16))
    span = TOKENS // blocks
    row_of = (to // span) * SUB + to % SUB
    row_at = (of // span) * SUB + of % SUB
    allowed = ((to // SUB) % (span // SUB) == (of // SUB) % (span // SUB)) & (row_at <= row_of)
    outs = []
    for g in range(TOKENS // span):
        mine = jnp.concatenate([y[g * span : (g + 1) * span] for y in regrouped], axis=0)
        across = []
        for h in range(heads):
            q, k, v = (mine[:, t * width + h * HD : t * width + (h + 1) * HD] for t in range(3))
            probs, total = softmax_rows(jnp.where(allowed, dot_nt(q, k), MASKED))
            across.append((dot_nn(probs, v) / total).astype(jnp.bfloat16))
        outs.append(jnp.concatenate(across, axis=1))
    for b in range(blocks):
        y = jnp.concatenate([o[b * span : (b + 1) * span] for o in outs], axis=0)
        z = dot_nn(back, y).astype(jnp.bfloat16)
        o_ref[b * SUB : (b + 1) * SUB] = z.reshape(SUB, COLS, width)


def column_attention(x):
    return pl.pallas_call(
        column_kernel,
        grid=(GROUP // AT_ONCE,),
        in_specs=[pl.BlockSpec((ROWS, 3 * COLS, AT_ONCE * HD), lambda h: (0, 0, h))],
        out_specs=pl.BlockSpec((ROWS, COLS, AT_ONCE * HD), lambda h: (0, 0, h)),
        out_shape=pltpu.HBM((ROWS, COLS, LOCAL), jnp.bfloat16),
        compiler_params=pltpu.CompilerParams(vmem_limit_bytes=SMALL_VMEM),
        cost_estimate=COST,
        name="column_attention",
    )(x)


TILE = 1024
TILES = WIDTH // TILE
CHUNK = 512
CHUNKS = WIDTH // CHUNK
WHOLE = pl.BlockSpec(memory_space=pltpu.VMEM)
ANYWHERE = pl.BlockSpec(memory_space=pl.ANY)


def own_rows_kernel(a_ref, w_ref, o_ref):
    o_ref[...] = dot_nn(a_ref[...], w_ref[...]).astype(jnp.bfloat16)


def project_own_rows(own, w_own):
    return pl.pallas_call(
        own_rows_kernel,
        grid=(TILES,),
        in_specs=[
            pl.BlockSpec((HALF, LOCAL), lambda n: (0, 0)),
            pl.BlockSpec((LOCAL, TILE), lambda n: (0, n)),
        ],
        out_specs=pl.BlockSpec((HALF, TILE), lambda n: (0, n)),
        out_shape=pltpu.HBM((HALF, WIDTH), jnp.bfloat16),
        compiler_params=pltpu.CompilerParams(vmem_limit_bytes=SMALL_VMEM),
        cost_estimate=COST,
        name="own_rows",
    )(in_hbm(own), in_hbm(w_own))


def head_of(s_ref, i):
    head = lax.bitwise_xor(2 * s_ref[1] + s_ref[2], i)
    return pl.ds(pl.multiple_of(head * HD, HD), HD)


def other_rows_kernel(s_ref, a_ref, acc_ref, *refs):
    pieces, o_ref, join_ref = refs[:4], refs[4], refs[5]

    @pl.when(pl.program_id(0) == 0)
    def _():
        for i in range(4):
            join_ref[:, i * HD : (i + 1) * HD] = a_ref[:, head_of(s_ref, i)]

    weights = jnp.concatenate([piece[...] for piece in pieces], axis=0)
    total = acc_ref[...].astype(jnp.float32) + dot_nn(join_ref[...], weights)
    o_ref[...] = total.astype(jnp.bfloat16)


def project_other_rows(place, other, acc, pieces):
    half = TILES // 2
    return pl.pallas_call(
        other_rows_kernel,
        grid_spec=pltpu.PrefetchScalarGridSpec(
            num_scalar_prefetch=1,
            grid=(half,),
            in_specs=[
                pl.BlockSpec((HALF, LOCAL), lambda n, s: (0, 0)),
                pl.BlockSpec((HALF, TILE), lambda n, s: (0, n + s[0] * half)),
                *[pl.BlockSpec((HD, TILE), lambda n, s: (0, n))] * 4,
            ],
            out_specs=pl.BlockSpec((HALF, TILE), lambda n, s: (0, n)),
            scratch_shapes=[pltpu.VMEM((HALF, LOCAL), jnp.bfloat16)],
        ),
        out_shape=pltpu.HBM((HALF, HALF_WIDTH), jnp.bfloat16),
        compiler_params=pltpu.CompilerParams(vmem_limit_bytes=SMALL_VMEM),
        cost_estimate=COST,
        name="other_rows",
    )(place, in_hbm(other), in_hbm(acc), *map(in_hbm, pieces))


def join_kernel(s_ref, x_ref, a_ref):
    me = s_ref[3]
    a_ref[:, :LOCAL] = x_ref[:, me].reshape(HALF, LOCAL)
    for i in range(4):
        other = x_ref[:, 1 - me, :, head_of(s_ref, i)].reshape(HALF, HD)
        a_ref[:, LOCAL + i * HD : LOCAL + (i + 1) * HD] = other


def join(place, attended):
    return pl.pallas_call(
        join_kernel,
        in_specs=[pl.BlockSpec(memory_space=pltpu.SMEM), WHOLE],
        out_specs=WHOLE,
        out_shape=jax.ShapeDtypeStruct((HALF, 2 * LOCAL), jnp.bfloat16),
        compiler_params=pltpu.CompilerParams(vmem_limit_bytes=SMALL_VMEM),
        cost_estimate=LONG,
        name="join",
    )(place, attended)


def project_kernel(s_ref, x_ref, y_ref, near_ref, far_ref, w_ref, *refs):
    pieces, o_ref = refs[:8], refs[8]
    a_buf, w_buf, acc_buf, o_buf, load_sems, store_sems, x_buf, row_sem = refs[9:]
    half = CHUNKS // 2
    depth = 2 * LOCAL

    def columns_of(n):
        at = lax.rem(n + s_ref[0] * half, CHUNKS)
        return pl.ds(pl.multiple_of(at * CHUNK, CHUNK), CHUNK)

    def loads_of(n):
        columns = columns_of(n)
        there = pl.ds(n % half * CHUNK, CHUNK)
        sems = load_sems.at[n]
        acc = near_ref.at[:, there] if n < half else far_ref.at[:, columns]
        copies = [
            (acc, acc_buf.at[n]),
            (w_ref.at[pl.ds(LOCAL, LOCAL), columns], w_buf.at[n, pl.ds(0, LOCAL)]),
        ]
        for i, piece in enumerate(pieces[:4] if n < half else pieces[4:]):
            to = w_buf.at[n, pl.ds(LOCAL + i * HD, HD)]
            copies.append((piece.at[pl.ds(HD, HD), there], to))
            if n >= half:
                to = w_buf.at[n, pl.ds(depth + i * HD, HD)]
                copies.append((piece.at[pl.ds(0, HD), there], to))
        return [pltpu.make_async_copy(*copy, sems.at[i]) for i, copy in enumerate(copies)]

    def store_of(n):
        return pltpu.make_async_copy(o_buf.at[n], o_ref.at[0, :, columns_of(n)], store_sems.at[n])

    rows = pltpu.make_async_copy(x_ref.at[pl.ds(0, HALF)], x_buf, row_sem)
    rows.start()
    for n in range(CHUNKS):
        for load in loads_of(n):
            load.start()
    for n in range(CHUNKS):
        for load in loads_of(n):
            load.wait()
        if n == half:
            rows.wait()
            for i in range(4):
                a_buf[:, i * HD : (i + 1) * HD] = x_buf[:, head_of(s_ref, i)]
        total = acc_buf[n].astype(jnp.float32) + dot_nn(y_ref[...], w_buf[n, :depth])
        if n >= half:
            total += dot_nn(a_buf[...], w_buf[n, depth:])
        o_buf[n] = total.astype(jnp.bfloat16)
        store_of(n).start()
    for n in range(CHUNKS):
        store_of(n).wait()


def project(place, row_other, joined, acc_near, acc, w_own, pieces):
    return pl.pallas_call(
        project_kernel,
        in_specs=[
            pl.BlockSpec(memory_space=pltpu.SMEM),
            ANYWHERE,
            WHOLE,
            *[ANYWHERE] * 11,
        ],
        out_specs=ANYWHERE,
        out_shape=pltpu.HBM((1, HALF, WIDTH), jnp.bfloat16),
        scratch_shapes=[
            pltpu.VMEM((HALF, LOCAL), jnp.bfloat16),
            pltpu.VMEM((CHUNKS, 3 * LOCAL, CHUNK), jnp.bfloat16),
            pltpu.VMEM((CHUNKS, HALF, CHUNK), jnp.bfloat16),
            pltpu.VMEM((CHUNKS, HALF, CHUNK), jnp.bfloat16),
            pltpu.SemaphoreType.DMA((CHUNKS, 10)),
            pltpu.SemaphoreType.DMA((CHUNKS,)),
            pltpu.VMEM((HALF, LOCAL), jnp.bfloat16),
            pltpu.SemaphoreType.DMA(()),
        ],
        compiler_params=pltpu.CompilerParams(vmem_limit_bytes=40 << 20),
        cost_estimate=COST,
        name="project",
    )(place, in_hbm(row_other), joined, *map(in_hbm, (acc_near, acc, w_own, *pieces)))


def slice_kernel(opposite, s_ref, w_ref, x_ref, buf, in_sems, out_sems):
    columns = pl.ds(pl.multiple_of(s_ref[0] * HALF_WIDTH, HALF_WIDTH), HALF_WIDTH)
    head = 2 * s_ref[1] + s_ref[2]
    if opposite:
        head = 3 - head
    loads, stores = [], []
    step = PIECE // SLICE_STEPS
    each = SLICE_STEPS // 2
    for n in range(SLICE_STEPS):
        start = pl.multiple_of(n // each * LOCAL + head * HD + n % each * step, step)
        at = pl.ds(n * step, step)
        loads.append(
            pltpu.make_async_copy(w_ref.at[pl.ds(start, step), columns], buf.at[at], in_sems.at[n])
        )
        stores.append(pltpu.make_async_copy(buf.at[at], x_ref.at[at], out_sems.at[n]))
    for load in loads:
        load.start()
    for load, store in zip(loads, stores):
        load.wait()
        store.start()
    for store in stores:
        store.wait()


SLICE_STEPS = 4


def slice_of(place, w_out, opposite):
    return pl.pallas_call(
        functools.partial(slice_kernel, opposite),
        in_specs=[pl.BlockSpec(memory_space=pltpu.SMEM), pl.BlockSpec(memory_space=pl.ANY)],
        out_specs=pl.BlockSpec(memory_space=pl.ANY),
        out_shape=pltpu.HBM((PIECE, HALF_WIDTH), jnp.bfloat16),
        scratch_shapes=[
            pltpu.VMEM((PIECE, HALF_WIDTH), jnp.bfloat16),
            pltpu.SemaphoreType.DMA((SLICE_STEPS,)),
            pltpu.SemaphoreType.DMA((SLICE_STEPS,)),
        ],
        compiler_params=pltpu.CompilerParams(vmem_limit_bytes=SMALL_VMEM),
        cost_estimate=COST,
        name="slice",
    )(place, in_hbm(w_out))


PACK_STEPS = 4


def pack_kernel(q_ref, k_ref, v_ref, o_ref, buf, in_sems, out_sems):
    step = ROWS // PACK_STEPS
    loads, stores = [], []
    for n in range(PACK_STEPS):
        at = pl.ds(n * step, step)
        loads.append(
            [
                pltpu.make_async_copy(
                    ref.at[0, half, at, :, pl.ds(LOCAL, LOCAL)],
                    buf.at[at, 2 * t + half],
                    in_sems.at[n, 2 * t + half],
                )
                for t, ref in enumerate((q_ref, k_ref, v_ref))
                for half in range(2)
            ]
        )
        stores.append(pltpu.make_async_copy(buf.at[at], o_ref.at[at], out_sems.at[n]))
    for group in loads:
        for load in group:
            load.start()
    for group, store in zip(loads, stores):
        for load in group:
            load.wait()
        store.start()
    for store in stores:
        store.wait()


def packed(*tensors):
    return pl.pallas_call(
        pack_kernel,
        in_specs=[pl.BlockSpec(memory_space=pl.ANY)] * 3,
        out_specs=pl.BlockSpec(memory_space=pl.ANY),
        out_shape=pltpu.HBM((ROWS, 6, 8, LOCAL), jnp.bfloat16),
        scratch_shapes=[
            pltpu.VMEM((ROWS, 6, 8, LOCAL), jnp.bfloat16),
            pltpu.SemaphoreType.DMA((PACK_STEPS, 6)),
            pltpu.SemaphoreType.DMA((PACK_STEPS,)),
        ],
        compiler_params=pltpu.CompilerParams(vmem_limit_bytes=SMALL_VMEM),
        cost_estimate=COST,
        name="pack",
    )(*[in_hbm(t.reshape(1, 2, ROWS, 8, 2 * LOCAL)) for t in tensors]).reshape(ROWS, 3 * COLS, LOCAL)


def on_device(queries, keys, values, w_out):
    place = jnp.stack([*position(), lax.axis_index("head")])
    piece, *col_qkv = lax.optimization_barrier(
        (slice_of(place, w_out, False), queries, keys, values)
    )
    mine = permute(piece, ALONG_X)
    sent = packed(*col_qkv)
    arrived = lax.all_to_all(sent, "ctx", split_axis=0, concat_axis=0, tiled=True)
    mine, w_late, *row_qkv = lax.optimization_barrier((mine, w_out, queries, keys, values))
    away = slice_of(place, w_late, True)
    row_own, row_away = row_attention(*row_qkv)
    acc = project_own_rows(row_own, w_out)
    mine, away, row_away, acc = lax.optimization_barrier((mine, away, row_away, acc))
    near = [mine, permute(mine, ALONG_Z), permute(mine, ALONG_Y), permute(away, ALONG_N)]
    row_other = permute(row_away, TO_HEAD)
    col = column_attention(arrived)
    near, row_other, _ = lax.optimization_barrier((near, row_other, col))
    far = [permute(piece, TO_CORE) for piece in near]
    col = col.reshape(2 * ROWS, 8, LOCAL)
    col = lax.all_to_all(col, ("ctx", "head"), split_axis=0, concat_axis=0, tiled=True)
    acc_near = project_other_rows(place, row_other, acc, near)
    col, acc_near = lax.optimization_barrier((col, acc_near))
    joined = join(place, col.reshape(ROWS, 2, 8, LOCAL))
    return project(place, row_other, joined, acc_near, acc, w_out, near + far)


def solution(mesh):
    return jax.shard_map(
        on_device,
        mesh=mesh,
        in_specs=(
            P("ctx", None, "head"),
            P("ctx", None, "head"),
            P("ctx", None, "head"),
            P("head", None),
        ),
        out_specs=P("ctx", "head", None),
        check_vma=False,
    )
```

```python
import functools
import itertools
import math

import jax
import jax.numpy as jnp
from jax import lax
from jax.experimental import pallas as pl
from jax.experimental.pallas import tpu as pltpu
from jax.sharding import PartitionSpec as P

HD = 128
GROUP = 4
LOCAL = GROUP * HD
LENGTH = 1024
ROWS = 64
HALF = LENGTH // 2
WIDTH = 4096
BLOCK = 256
SCALE = math.log2(math.e) / math.sqrt(HD)
MASKED = -1e30
SMALL_VMEM = 16 << 20
COST = pl.CostEstimate(flops=1 << 20, transcendentals=0, bytes_accessed=1 << 10)
LONG = pl.CostEstimate(flops=1 << 38, transcendentals=0, bytes_accessed=1 << 20)

PLACES = list(itertools.product(range(4), range(4), range(4), range(2)))
HALF_WIDTH = WIDTH // 2
PIECE = LENGTH // 4


def index_of(x, y, z, core):
    return (((z % 4) * 2 + (x % 4) // 2) * 4 + y % 4) * 4 + core * 2 + x % 2


def pair(at, core):
    return at + 1 if at % 2 == core else at - 1


def moves(step):
    return [(index_of(*place), index_of(*step(*place))) for place in PLACES]


ALONG_X = moves(lambda x, y, z, core: (x + 1 - 2 * core, y, z, core))
ALONG_Y = moves(lambda x, y, z, core: (x, pair(y, core), z, core))
ALONG_Z = moves(lambda x, y, z, core: (x, y, pair(z, core), core))
ALONG_N = moves(lambda x, y, z, core: (x - 1 + 2 * (x % 2), y, z, core))
TO_CORE = moves(lambda x, y, z, core: (x, y, z, 1 - core))
TO_HEAD = moves(lambda x, y, z, core: (x + 1 - 2 * (x % 2), y, z, core))


def position():
    ctx = lax.axis_index("ctx")
    return ctx & 1, (ctx >> 1) & 1, (ctx >> 4) & 1


def permute(x, pairs):
    return lax.ppermute(x, ("ctx", "head"), pairs)


def in_hbm(x):
    return pltpu.with_memory_space_constraint(x, pltpu.HBM)


def softmax_rows(scores):
    top = jnp.max(scores, axis=-1, keepdims=True)
    expo = jnp.exp2((scores - top) * SCALE)
    total = jnp.sum(expo, axis=-1, keepdims=True)
    return expo.astype(jnp.bfloat16), total


def dot_nt(a, b):
    return lax.dot_general(a, b, (((1,), (1,)), ((), ())), preferred_element_type=jnp.float32)


def dot_nn(a, b):
    return jnp.dot(a, b, preferred_element_type=jnp.float32)


def row_kernel(q_ref, k_ref, v_ref, own_ref, other_ref):
    me = lax.axis_index("head")
    lower = lax.broadcasted_iota(jnp.int32, (BLOCK, BLOCK), 1) <= lax.broadcasted_iota(
        jnp.int32, (BLOCK, BLOCK), 0
    )
    per_half = HALF // BLOCK
    other_ref[HALF:] = jnp.zeros((HALF, HD), jnp.bfloat16)
    for i in range(LENGTH // BLOCK):
        q = q_ref[0, i * BLOCK : (i + 1) * BLOCK, :]
        end = (i + 1) * BLOCK
        diag = jnp.where(lower, dot_nt(q, k_ref[0, i * BLOCK : end, :]), MASKED)
        if i:
            scores = jnp.concatenate([dot_nt(q, k_ref[0, : i * BLOCK, :]), diag], axis=1)
        else:
            scores = diag
        probs, total = softmax_rows(scores)
        out = (dot_nn(probs, v_ref[0, :end, :]) / total).astype(jnp.bfloat16)
        at = pl.ds((i % per_half) * BLOCK, BLOCK)

        @pl.when(me == i // per_half)
        def _():
            own_ref[at, :] = out

        @pl.when(me != i // per_half)
        def _():
            other_ref[at, :] = out


def row_attention(queries, keys, values):
    spec = pl.BlockSpec((1, LENGTH, HD), lambda h: (0, 0, h))
    return pl.pallas_call(
        row_kernel,
        grid=(GROUP,),
        in_specs=[spec] * 3,
        out_specs=[
            pl.BlockSpec((HALF, HD), lambda h: (0, h)),
            pl.BlockSpec((2 * HALF, HD), lambda h: (0, h)),
        ],
        out_shape=[
            pltpu.HBM((HALF, LOCAL), jnp.bfloat16),
            pltpu.HBM((2 * HALF, LOCAL), jnp.bfloat16),
        ],
        compiler_params=pltpu.CompilerParams(vmem_limit_bytes=SMALL_VMEM),
        cost_estimate=LONG,
        name="row_attention",
    )(in_hbm(queries), in_hbm(keys), in_hbm(values))


COLS = 16
SUB = 16
TOKENS = SUB * COLS
AT_ONCE = 2


def column_kernel(x_ref, o_ref):
    to = lax.broadcasted_iota(jnp.int32, (TOKENS, TOKENS), 0)
    of = lax.broadcasted_iota(jnp.int32, (TOKENS, TOKENS), 1)
    swap = ((to % SUB) * COLS + to // SUB == of).astype(jnp.bfloat16)
    back = ((to % COLS) * SUB + to // COLS == of).astype(jnp.bfloat16)
    blocks = ROWS // SUB
    heads = o_ref.shape[2] // HD
    width = heads * HD
    regrouped = []
    for b in range(blocks):
        x = x_ref[b * SUB : (b + 1) * SUB]
        parts = [x[:, t * COLS : (t + 1) * COLS, :].reshape(TOKENS, width) for t in range(3)]
        regrouped.append(dot_nn(swap, jnp.concatenate(parts, axis=1)).astype(jnp.bfloat16))
    span = TOKENS // blocks
    row_of = (to // span) * SUB + to % SUB
    row_at = (of // span) * SUB + of % SUB
    allowed = ((to // SUB) % (span // SUB) == (of // SUB) % (span // SUB)) & (row_at <= row_of)
    outs = []
    for g in range(TOKENS // span):
        mine = jnp.concatenate([y[g * span : (g + 1) * span] for y in regrouped], axis=0)
        across = []
        for h in range(heads):
            q, k, v = (mine[:, t * width + h * HD : t * width + (h + 1) * HD] for t in range(3))
            probs, total = softmax_rows(jnp.where(allowed, dot_nt(q, k), MASKED))
            across.append((dot_nn(probs, v) / total).astype(jnp.bfloat16))
        outs.append(jnp.concatenate(across, axis=1))
    for b in range(blocks):
        y = jnp.concatenate([o[b * span : (b + 1) * span] for o in outs], axis=0)
        z = dot_nn(back, y).astype(jnp.bfloat16)
        o_ref[b * SUB : (b + 1) * SUB] = z.reshape(SUB, COLS, width)


def column_attention(x):
    return pl.pallas_call(
        column_kernel,
        grid=(GROUP // AT_ONCE,),
        in_specs=[pl.BlockSpec((ROWS, 3 * COLS, AT_ONCE * HD), lambda h: (0, 0, h))],
        out_specs=pl.BlockSpec((ROWS, COLS, AT_ONCE * HD), lambda h: (0, 0, h)),
        out_shape=pltpu.HBM((ROWS, COLS, LOCAL), jnp.bfloat16),
        compiler_params=pltpu.CompilerParams(vmem_limit_bytes=SMALL_VMEM),
        cost_estimate=COST,
        name="column_attention",
    )(x)


TILE = 1024
TILES = WIDTH // TILE
CHUNK = 512
CHUNKS = WIDTH // CHUNK
WHOLE = pl.BlockSpec(memory_space=pltpu.VMEM)
ANYWHERE = pl.BlockSpec(memory_space=pl.ANY)


def own_rows_kernel(a_ref, w_ref, o_ref):
    o_ref[...] = dot_nn(a_ref[...], w_ref[...]).astype(jnp.bfloat16)


def project_own_rows(own, w_own):
    return pl.pallas_call(
        own_rows_kernel,
        grid=(TILES,),
        in_specs=[
            pl.BlockSpec((HALF, LOCAL), lambda n: (0, 0)),
            pl.BlockSpec((LOCAL, TILE), lambda n: (0, n)),
        ],
        out_specs=pl.BlockSpec((HALF, TILE), lambda n: (0, n)),
        out_shape=pltpu.HBM((HALF, WIDTH), jnp.bfloat16),
        compiler_params=pltpu.CompilerParams(vmem_limit_bytes=SMALL_VMEM),
        cost_estimate=COST,
        name="own_rows",
    )(in_hbm(own), in_hbm(w_own))


def head_of(s_ref, i):
    head = lax.bitwise_xor(2 * s_ref[1] + s_ref[2], i)
    return pl.ds(pl.multiple_of(head * HD, HD), HD)


def other_rows_kernel(s_ref, a_ref, acc_ref, *refs):
    pieces, o_ref, join_ref = refs[:4], refs[4], refs[5]

    @pl.when(pl.program_id(0) == 0)
    def _():
        for i in range(4):
            join_ref[:, i * HD : (i + 1) * HD] = a_ref[:, head_of(s_ref, i)]

    weights = jnp.concatenate([piece[...] for piece in pieces], axis=0)
    total = acc_ref[...].astype(jnp.float32) + dot_nn(join_ref[...], weights)
    o_ref[...] = total.astype(jnp.bfloat16)


def project_other_rows(place, other, acc, pieces):
    half = TILES // 2
    return pl.pallas_call(
        other_rows_kernel,
        grid_spec=pltpu.PrefetchScalarGridSpec(
            num_scalar_prefetch=1,
            grid=(half,),
            in_specs=[
                pl.BlockSpec((HALF, LOCAL), lambda n, s: (0, 0)),
                pl.BlockSpec((HALF, TILE), lambda n, s: (0, n + s[0] * half)),
                *[pl.BlockSpec((HD, TILE), lambda n, s: (0, n))] * 4,
            ],
            out_specs=pl.BlockSpec((HALF, TILE), lambda n, s: (0, n)),
            scratch_shapes=[pltpu.VMEM((HALF, LOCAL), jnp.bfloat16)],
        ),
        out_shape=pltpu.HBM((HALF, HALF_WIDTH), jnp.bfloat16),
        compiler_params=pltpu.CompilerParams(vmem_limit_bytes=SMALL_VMEM),
        cost_estimate=COST,
        name="other_rows",
    )(place, in_hbm(other), in_hbm(acc), *map(in_hbm, pieces))


def join_kernel(s_ref, x_ref, a_ref):
    me = s_ref[3]
    a_ref[:, :LOCAL] = x_ref[:, me].reshape(HALF, LOCAL)
    for i in range(4):
        other = x_ref[:, 1 - me, :, head_of(s_ref, i)].reshape(HALF, HD)
        a_ref[:, LOCAL + i * HD : LOCAL + (i + 1) * HD] = other


def join(place, attended):
    return pl.pallas_call(
        join_kernel,
        in_specs=[pl.BlockSpec(memory_space=pltpu.SMEM), WHOLE],
        out_specs=WHOLE,
        out_shape=jax.ShapeDtypeStruct((HALF, 2 * LOCAL), jnp.bfloat16),
        compiler_params=pltpu.CompilerParams(vmem_limit_bytes=SMALL_VMEM),
        cost_estimate=LONG,
        name="join",
    )(place, attended)


def project_kernel(s_ref, x_ref, y_ref, near_ref, far_ref, w_ref, *refs):
    pieces, o_ref = refs[:8], refs[8]
    a_buf, w_buf, acc_buf, o_buf, load_sems, store_sems = refs[9:]
    half = CHUNKS // 2
    depth = 2 * LOCAL

    def columns_of(n):
        at = lax.rem(n + s_ref[0] * half, CHUNKS)
        return pl.ds(pl.multiple_of(at * CHUNK, CHUNK), CHUNK)

    def loads_of(n):
        columns = columns_of(n)
        there = pl.ds(n % half * CHUNK, CHUNK)
        sems = load_sems.at[n]
        acc = near_ref.at[:, there] if n < half else far_ref.at[:, columns]
        copies = [
            (acc, acc_buf.at[n]),
            (w_ref.at[pl.ds(LOCAL, LOCAL), columns], w_buf.at[n, pl.ds(0, LOCAL)]),
        ]
        for i, piece in enumerate(pieces[:4] if n < half else pieces[4:]):
            to = w_buf.at[n, pl.ds(LOCAL + i * HD, HD)]
            copies.append((piece.at[pl.ds(HD, HD), there], to))
            if n >= half:
                to = w_buf.at[n, pl.ds(depth + i * HD, HD)]
                copies.append((piece.at[pl.ds(0, HD), there], to))
        return [pltpu.make_async_copy(*copy, sems.at[i]) for i, copy in enumerate(copies)]

    def store_of(n):
        return pltpu.make_async_copy(o_buf.at[n], o_ref.at[0, :, columns_of(n)], store_sems.at[n])

    for n in range(CHUNKS):
        for load in loads_of(n):
            load.start()
    for i in range(4):
        a_buf[:, i * HD : (i + 1) * HD] = x_ref[:HALF, head_of(s_ref, i)]
    for n in range(CHUNKS):
        for load in loads_of(n):
            load.wait()
        total = acc_buf[n].astype(jnp.float32) + dot_nn(y_ref[...], w_buf[n, :depth])
        if n >= half:
            total += dot_nn(a_buf[...], w_buf[n, depth:])
        o_buf[n] = total.astype(jnp.bfloat16)
        store_of(n).start()
    for n in range(CHUNKS):
        store_of(n).wait()


def project(place, row_other, joined, acc_near, acc, w_own, pieces):
    return pl.pallas_call(
        project_kernel,
        in_specs=[
            pl.BlockSpec(memory_space=pltpu.SMEM),
            WHOLE,
            WHOLE,
            *[ANYWHERE] * 11,
        ],
        out_specs=ANYWHERE,
        out_shape=pltpu.HBM((1, HALF, WIDTH), jnp.bfloat16),
        scratch_shapes=[
            pltpu.VMEM((HALF, LOCAL), jnp.bfloat16),
            pltpu.VMEM((CHUNKS, 3 * LOCAL, CHUNK), jnp.bfloat16),
            pltpu.VMEM((CHUNKS, HALF, CHUNK), jnp.bfloat16),
            pltpu.VMEM((CHUNKS, HALF, CHUNK), jnp.bfloat16),
            pltpu.SemaphoreType.DMA((CHUNKS, 10)),
            pltpu.SemaphoreType.DMA((CHUNKS,)),
        ],
        compiler_params=pltpu.CompilerParams(vmem_limit_bytes=40 << 20),
        cost_estimate=COST,
        name="project",
    )(place, row_other, joined, *map(in_hbm, (acc_near, acc, w_own, *pieces)))


def slice_kernel(opposite, s_ref, w_ref, x_ref, buf, in_sems, out_sems):
    columns = pl.ds(pl.multiple_of(s_ref[0] * HALF_WIDTH, HALF_WIDTH), HALF_WIDTH)
    head = 2 * s_ref[1] + s_ref[2]
    if opposite:
        head = 3 - head
    loads, stores = [], []
    step = PIECE // SLICE_STEPS
    each = SLICE_STEPS // 2
    for n in range(SLICE_STEPS):
        start = pl.multiple_of(n // each * LOCAL + head * HD + n % each * step, step)
        at = pl.ds(n * step, step)
        loads.append(
            pltpu.make_async_copy(w_ref.at[pl.ds(start, step), columns], buf.at[at], in_sems.at[n])
        )
        stores.append(pltpu.make_async_copy(buf.at[at], x_ref.at[at], out_sems.at[n]))
    for load in loads:
        load.start()
    for load, store in zip(loads, stores):
        load.wait()
        store.start()
    for store in stores:
        store.wait()


SLICE_STEPS = 4


def slice_of(place, w_out, opposite):
    return pl.pallas_call(
        functools.partial(slice_kernel, opposite),
        in_specs=[pl.BlockSpec(memory_space=pltpu.SMEM), pl.BlockSpec(memory_space=pl.ANY)],
        out_specs=pl.BlockSpec(memory_space=pl.ANY),
        out_shape=pltpu.HBM((PIECE, HALF_WIDTH), jnp.bfloat16),
        scratch_shapes=[
            pltpu.VMEM((PIECE, HALF_WIDTH), jnp.bfloat16),
            pltpu.SemaphoreType.DMA((SLICE_STEPS,)),
            pltpu.SemaphoreType.DMA((SLICE_STEPS,)),
        ],
        compiler_params=pltpu.CompilerParams(vmem_limit_bytes=SMALL_VMEM),
        cost_estimate=COST,
        name="slice",
    )(place, in_hbm(w_out))


PACK_STEPS = 4


def pack_kernel(q_ref, k_ref, v_ref, o_ref, buf, in_sems, out_sems):
    step = ROWS // PACK_STEPS
    loads, stores = [], []
    for n in range(PACK_STEPS):
        at = pl.ds(n * step, step)
        loads.append(
            [
                pltpu.make_async_copy(
                    ref.at[0, half, at, :, pl.ds(LOCAL, LOCAL)],
                    buf.at[at, 2 * t + half],
                    in_sems.at[n, 2 * t + half],
                )
                for t, ref in enumerate((q_ref, k_ref, v_ref))
                for half in range(2)
            ]
        )
        stores.append(pltpu.make_async_copy(buf.at[at], o_ref.at[at], out_sems.at[n]))
    for group in loads:
        for load in group:
            load.start()
    for group, store in zip(loads, stores):
        for load in group:
            load.wait()
        store.start()
    for store in stores:
        store.wait()


def packed(*tensors):
    return pl.pallas_call(
        pack_kernel,
        in_specs=[pl.BlockSpec(memory_space=pl.ANY)] * 3,
        out_specs=pl.BlockSpec(memory_space=pl.ANY),
        out_shape=pltpu.HBM((ROWS, 6, 8, LOCAL), jnp.bfloat16),
        scratch_shapes=[
            pltpu.VMEM((ROWS, 6, 8, LOCAL), jnp.bfloat16),
            pltpu.SemaphoreType.DMA((PACK_STEPS, 6)),
            pltpu.SemaphoreType.DMA((PACK_STEPS,)),
        ],
        compiler_params=pltpu.CompilerParams(vmem_limit_bytes=SMALL_VMEM),
        cost_estimate=COST,
        name="pack",
    )(*[in_hbm(t.reshape(1, 2, ROWS, 8, 2 * LOCAL)) for t in tensors]).reshape(ROWS, 3 * COLS, LOCAL)


def on_device(queries, keys, values, w_out):
    place = jnp.stack([*position(), lax.axis_index("head")])
    piece, *col_qkv = lax.optimization_barrier(
        (slice_of(place, w_out, False), queries, keys, values)
    )
    mine = permute(piece, ALONG_X)
    sent = packed(*col_qkv)
    arrived = lax.all_to_all(sent, "ctx", split_axis=0, concat_axis=0, tiled=True)
    mine, w_late, *row_qkv = lax.optimization_barrier((mine, w_out, queries, keys, values))
    away = slice_of(place, w_late, True)
    row_own, row_away = row_attention(*row_qkv)
    acc = project_own_rows(row_own, w_out)
    mine, away, row_away, acc = lax.optimization_barrier((mine, away, row_away, acc))
    near = [mine, permute(mine, ALONG_Z), permute(mine, ALONG_Y), permute(away, ALONG_N)]
    row_other = permute(row_away, TO_HEAD)
    col = column_attention(arrived)
    near, row_other, _ = lax.optimization_barrier((near, row_other, col))
    far = [permute(piece, TO_CORE) for piece in near]
    col = col.reshape(2 * ROWS, 8, LOCAL)
    col = lax.all_to_all(col, ("ctx", "head"), split_axis=0, concat_axis=0, tiled=True)
    acc_near = project_other_rows(place, row_other, acc, near)
    col, acc_near = lax.optimization_barrier((col, acc_near))
    joined = join(place, col.reshape(ROWS, 2, 8, LOCAL))
    return project(place, row_other, joined, acc_near, acc, w_out, near + far)


def solution(mesh):
    return jax.shard_map(
        on_device,
        mesh=mesh,
        in_specs=(
            P("ctx", None, "head"),
            P("ctx", None, "head"),
            P("ctx", None, "head"),
            P("head", None),
        ),
        out_specs=P("ctx", "head", None),
        check_vma=False,
    )
```
